256 devices in a mesh: bl: 32 (over x, z), ta: 8 (over y, core).
Axes of the slice: x: 4, y: 4, z: 8, core: 2. Of those that a mesh axis runs over, the one named last changes fastest.
Arguments:
- log_amplitude: bfloat16 [8192, 8, 1536], P('bl', 'ta'), may hold values from -2.5 to 2.5
- phase: bfloat16 [8192, 8, 1536], P('bl', 'ta'), may hold values from -4 to 4
- redundant_group_index: int32 [8192], P('bl'), may hold values from 0 to 223, as said below
- antenna_couples: int32 [8192, 2], P('bl'), may hold values from 0 to 349, as said below
- tile_flag_mask: int32 [8192, 12], P(('bl', 'ta')), may hold values from 0 to 1, as said below
- inverse: float32 [2, 350, 350], replicated, may hold values from -1 to 1
- integration_kernel: float32 [8, 8], replicated, may hold values from 0.01 to 1
- channel_kernel: bfloat16 [7, 128, 128], replicated, may hold values from 0.0009994507 to 1
Outputs:
- antenna_gains: float32 [2, 350, 8, 1536], P(None, None, 'ta')
- filled: float32 [2, 8192, 8, 1536], P(None, ('bl', 'ta'))
The draws below stay inside these ranges and needn't reach their ends.
Inputs may be any that keep to these rules, and one draw needn't show every extreme that they name: `redundant_group_index`: every group from 0 to 223 holds at least one baseline. `antenna_couples`: the two antennas of a baseline differ. `tile_flag_mask`: both neighbouring tiles of a flagged tile are unflagged.
All inputs are finite; a program needn't handle non-finite values.
Results may differ from the reference program's by a relative error of at most 0.0029.
Values may be sent and summed in bfloat16 or wider, within the bound.
A program may use at most 64 MiB of HBM per device.

```python
import math
import jax
import jax.numpy as jnp
from jax import lax

ANTENNA_COUNT = 350
F = 1536
TILE = 128
REACH = 3
NGRP = 224
BL_DEV = 256
BASELINE_TOTAL = 8192
TIMES = 8
NTILE = 12
N_TA = 8


def draw_redundant_group_index(key, part):
    order_key = jax.random.fold_in(key, 101)
    left_key = jax.random.fold_in(key, 102)
    right_key = jax.random.fold_in(key, 103)
    order = jax.random.permutation(order_key, BASELINE_TOTAL).astype(jnp.int32)
    left_part = jax.random.randint(left_key, (BASELINE_TOTAL,), 0, NGRP, dtype=jnp.int32)
    right_part = jax.random.randint(right_key, (BASELINE_TOTAL,), 0, NGRP, dtype=jnp.int32)
    skewed = left_part * right_part // NGRP
    return jnp.where(order < NGRP, order, skewed).astype(jnp.int32)


def draw_antenna_couples(key, part):
    first_random_key = jax.random.fold_in(key, 201)
    step_key = jax.random.fold_in(key, 202)
    first_antenna = jax.random.randint(first_random_key, (BASELINE_TOTAL,), 0, ANTENNA_COUNT, dtype=jnp.int32)
    step_spacing = jax.random.randint(step_key, (BASELINE_TOTAL,), 1, ANTENNA_COUNT, dtype=jnp.int32)
    second_antenna = (first_antenna + step_spacing) % ANTENNA_COUNT
    return jnp.stack([first_antenna, second_antenna], axis=1).astype(jnp.int32)


def draw_tile_flag_mask(key, part):
    rate_key = jax.random.fold_in(key, 301)
    raw_key = jax.random.fold_in(key, 302)
    rates = jax.random.randint(rate_key, (BASELINE_TOTAL, 1), 0, 4, dtype=jnp.int32)
    rolls = jax.random.randint(raw_key, (BASELINE_TOTAL, NTILE), 0, 8, dtype=jnp.int32)
    marked = (rolls < rates).astype(jnp.int32)
    before = jnp.pad(marked[:, :-1], ((0, 0), (1, 0)))
    return (marked * (1 - before)).astype(jnp.int32)


def draw_inverse(key, part):
    off_key = jax.random.fold_in(key, 401)
    diag_key = jax.random.fold_in(key, 402)
    identity = jnp.eye(ANTENNA_COUNT, dtype=jnp.float32)
    off_diag = jnp.clip(jax.random.normal(off_key, (2, ANTENNA_COUNT, ANTENNA_COUNT), jnp.float32), -4.0, 4.0) * (0.06 / math.sqrt(ANTENNA_COUNT))
    diagonal = jax.random.uniform(diag_key, (2, ANTENNA_COUNT), jnp.float32, 0.05, 0.15)
    return off_diag * (1.0 - identity) + diagonal[:, :, None] * identity


def level_of(stream_key, shape, cuts, least, high):
    level = 1.0
    for axis_at, parts in cuts:
        heights = jax.random.uniform(jax.random.fold_in(jax.random.fold_in(stream_key, 6), axis_at), (parts,), jnp.float32, least / len(cuts), high / len(cuts))
        level = level * jnp.repeat(jnp.exp(heights), shape[axis_at] // parts).reshape((-1,) + (1,) * (len(shape) - 1 - axis_at))
    return level


def scatter_about(rng, shape, spread, most, split=(), kind=jnp.bfloat16):
    drawn = spread * jax.random.normal(rng, shape, jnp.float32)
    if split:
        drawn = drawn * level_of(rng, shape, split, -0.22, 0.18)
    return jnp.clip(drawn, -most, most).astype(kind)


def setup_inputs(seed: int = 0) -> dict:
    keys = jax.random.split(jax.random.key(seed), 9)
    return {
        "log_amplitude": scatter_about(keys[0], (BASELINE_TOTAL, TIMES, F), 0.35, 2.5, ((0, 32), (1, 8))),
        "phase": scatter_about(keys[1], (BASELINE_TOTAL, TIMES, F), 1.0, 4.0, ((0, 32), (1, 8))),
        "redundant_group_index": draw_redundant_group_index(jax.random.fold_in(keys[8], 71), 0),
        "antenna_couples": draw_antenna_couples(jax.random.fold_in(keys[8], 71), 0),
        "tile_flag_mask": draw_tile_flag_mask(jax.random.fold_in(keys[8], 71), 0),
        "inverse": draw_inverse(jax.random.fold_in(keys[8], 71), 0),
        "integration_kernel": jnp.clip(jnp.exp(jax.random.uniform(keys[6], (TIMES, TIMES), jnp.float32, math.log(0.01), math.log(1.0))), 0.01, 1.0),
        "channel_kernel": jnp.clip(jnp.exp(jax.random.uniform(keys[7], (2 * REACH + 1, TILE, TILE), jnp.float32, math.log(0.0009994507), math.log(1.0))), 0.0009994507, 1.0).astype(jnp.bfloat16),
    }


def mix_channels(values, channel_kernel):
    span_tiles = (channel_kernel.shape[0] - 1) // 2
    tile_width = channel_kernel.shape[1]
    leading = values.shape[:-1]
    tile_count = values.shape[-1] // tile_width
    tiled = values.reshape(leading + (tile_count, tile_width)).astype(jnp.float32)
    pad_spec = [(0, 0)] * len(leading) + [(span_tiles, span_tiles), (0, 0)]
    padded = jnp.pad(tiled, pad_spec)
    summed = jnp.zeros(leading + (tile_count, tile_width), jnp.float32)
    for offset in range(2 * span_tiles + 1):
        window = lax.slice_in_dim(padded, offset, offset + tile_count, axis=len(leading))
        summed = summed + jnp.einsum("...kj,ij->...ki", window, channel_kernel[offset].astype(jnp.float32),
                                     precision=lax.Precision.HIGHEST)
    return summed.reshape(leading + (tile_count * tile_width,))


def fill_block(calibrated, tile_flag_mask, integration_kernel, channel_kernel):
    tile_width = channel_kernel.shape[1]
    weight = jnp.repeat((1 - tile_flag_mask).astype(jnp.bfloat16), tile_width, axis=1)
    masked = calibrated * weight[None, :, None, :]
    mixed = mix_channels(masked, channel_kernel)
    numerator = jnp.einsum("tu,kbuf->kbtf", integration_kernel, mixed, precision=lax.Precision.HIGHEST)
    weight_mix = mix_channels(weight, channel_kernel)
    denominator = jnp.sum(integration_kernel, axis=1)[None, :, None] * weight_mix[:, None, :]
    keep = weight.astype(jnp.float32)[None, :, None, :]
    return keep * calibrated.astype(jnp.float32) + (1.0 - keep) * numerator / denominator[None]


def reference(log_amplitude, phase, redundant_group_index, antenna_couples, tile_flag_mask, inverse, integration_kernel, channel_kernel):
    first_antenna = antenna_couples[:, 0]
    second_antenna = antenna_couples[:, 1]
    group_counts = jax.ops.segment_sum(jnp.ones((BASELINE_TOTAL,), jnp.float32), redundant_group_index, num_segments=NGRP)
    sign_reversal = jnp.array([1.0, -1.0], dtype=jnp.float32)

    def per_time(rows):
        amp_rows, phase_rows = rows
        stacked_terms = jnp.stack([amp_rows, phase_rows], axis=1).astype(jnp.float32)
        group_mean = jax.ops.segment_sum(stacked_terms, redundant_group_index, num_segments=NGRP) / group_counts[:, None, None]
        fit_residual = stacked_terms - group_mean[redundant_group_index]
        normal_right_side = jax.ops.segment_sum(fit_residual, first_antenna, num_segments=ANTENNA_COUNT)
        normal_right_side = normal_right_side + sign_reversal[None, :, None] * jax.ops.segment_sum(fit_residual, second_antenna, num_segments=ANTENNA_COUNT)
        gain_terms = jnp.einsum("sab,bsf->saf", inverse, normal_right_side, precision=lax.Precision.HIGHEST)
        amplitude_gain = gain_terms[0]
        phase_gain_term = gain_terms[1]
        calibrated_amplitude = stacked_terms[:, 0] - amplitude_gain[first_antenna] - amplitude_gain[second_antenna]
        calibrated_phase = stacked_terms[:, 1] - phase_gain_term[first_antenna] + phase_gain_term[second_antenna]
        magnitude = jnp.exp(calibrated_amplitude)
        calibrated = jnp.stack([magnitude * jnp.cos(calibrated_phase), magnitude * jnp.sin(calibrated_phase)]).astype(jnp.bfloat16)
        return gain_terms, calibrated

    gain_time, cal_time = lax.map(per_time, (jnp.swapaxes(log_amplitude, 0, 1), jnp.swapaxes(phase, 0, 1)))
    antenna_gains = jnp.transpose(gain_time, (1, 2, 0, 3))
    calibrated = jnp.transpose(cal_time, (1, 2, 0, 3))
    block_rows = BL_DEV // N_TA
    block_count = BASELINE_TOTAL // block_rows
    cal_blocks = jnp.transpose(calibrated.reshape(2, block_count, block_rows, TIMES, F), (1, 0, 2, 3, 4))
    flag_blocks = tile_flag_mask.reshape(block_count, block_rows, NTILE)

    def one_block(pair):
        return fill_block(pair[0], pair[1], integration_kernel, channel_kernel)

    filled_blocks = lax.map(one_block, (cal_blocks, flag_blocks))
    filled = jnp.transpose(filled_blocks, (1, 0, 2, 3, 4)).reshape(2, BASELINE_TOTAL, TIMES, F)
    return antenna_gains, filled
```

```python
import jax
import jax.numpy as jnp
from jax import lax
from jax.sharding import PartitionSpec as P

ANTENNA_COUNT = 350
NGRP = 224
TILE = 128
REACH = 3
HIGH = lax.Precision.HIGHEST


def mix_channels(values, channel_kernel):
    leading = values.shape[:-1]
    tile_count = values.shape[-1] // TILE
    tiled = values.reshape(leading + (tile_count, TILE))
    pad_spec = [(0, 0)] * len(leading) + [(REACH, REACH), (0, 0)]
    padded = jnp.pad(tiled, pad_spec)
    summed = jnp.zeros(leading + (tile_count, TILE), jnp.float32)
    for offset in range(2 * REACH + 1):
        window = lax.slice_in_dim(padded, offset, offset + tile_count, axis=len(leading))
        summed = summed + jnp.einsum(
            "...kj,ij->...ki", window, channel_kernel[offset], preferred_element_type=jnp.float32
        )
    return summed.reshape(leading + (tile_count * TILE,))


def fill_block(calibrated, tile_flag_mask, integration_kernel, channel_kernel):
    weight = jnp.repeat((1 - tile_flag_mask).astype(jnp.bfloat16), TILE, axis=1)
    masked = calibrated * weight[None, :, None, :]
    mixed = mix_channels(masked, channel_kernel)
    numerator = jnp.einsum("tu,kbuf->kbtf", integration_kernel, mixed, precision=HIGH)
    weight_mix = mix_channels(weight, channel_kernel)
    denominator = jnp.sum(integration_kernel, axis=1)[None, :, None] * weight_mix[:, None, :]
    keep = weight.astype(jnp.float32)[None, :, None, :]
    return keep * calibrated.astype(jnp.float32) + (1.0 - keep) * numerator / denominator[None]


def on_device(
    log_amplitude,
    phase,
    redundant_group_index,
    antenna_couples,
    tile_flag_mask,
    inverse,
    integration_kernel,
    channel_kernel,
):
    n_bl = lax.axis_size("bl")
    rows, _, chans = log_amplitude.shape
    own = chans // n_bl
    data = jnp.stack([log_amplitude[:, 0], phase[:, 0]])
    blocks = data.reshape(2, rows, n_bl, own).transpose(2, 0, 3, 1)
    got = lax.all_to_all(blocks, "bl", split_axis=0, concat_axis=0, tiled=True)
    index = jnp.concatenate([redundant_group_index[:, None], antenna_couples], axis=1)
    index = lax.all_gather(index.T, "bl", axis=0, tiled=False)
    index = index.transpose(1, 0, 2).reshape(3, n_bl * rows)
    group_hot = (index[0][None, :] == jnp.arange(NGRP, dtype=jnp.int32)[:, None]).astype(jnp.bfloat16)
    labels = jnp.arange(ANTENNA_COUNT, dtype=jnp.int32)[:, None]
    first = (index[1][None, :] == labels).astype(jnp.bfloat16)
    second = (index[2][None, :] == labels).astype(jnp.bfloat16)
    signed = jnp.stack([first + second, first - second])
    wide = got.transpose(1, 2, 0, 3).reshape(2, own, n_bl * rows)
    group_sums = jnp.einsum("sfb,gb->sgf", wide, group_hot, preferred_element_type=jnp.float32)
    antenna_sums = jnp.einsum("sfb,sab->saf", wide, signed, preferred_element_type=jnp.float32)
    cross = jnp.einsum("sab,gb->sag", signed, group_hot, preferred_element_type=jnp.float32)
    counts = jnp.sum(group_hot.astype(jnp.float32), axis=1)
    group_mean = group_sums / counts[None, :, None]
    rhs = antenna_sums - jnp.einsum("sag,sgf->saf", cross, group_mean, precision=HIGH)
    gains = jnp.einsum("sab,sbf->saf", inverse, rhs, precision=HIGH)
    antenna_gains = lax.all_gather(gains, "bl", axis=2, tiled=True)

    first_local = antenna_couples[:, 0]
    second_local = antenna_couples[:, 1]
    amp, ph = antenna_gains[0], antenna_gains[1]
    u = data[0].astype(jnp.float32) - amp[first_local] - amp[second_local]
    v = data[1].astype(jnp.float32) - ph[first_local] + ph[second_local]
    magnitude = jnp.exp(u)
    calibrated = jnp.stack([magnitude * jnp.cos(v), magnitude * jnp.sin(v)]).astype(jnp.bfloat16)
    filled = fill_block(
        lax.all_to_all(calibrated[:, :, None], "ta", split_axis=1, concat_axis=2, tiled=True),
        tile_flag_mask,
        integration_kernel,
        channel_kernel,
    )
    return (antenna_gains[:, :, None], filled)


def solution(mesh):
    in_specs = (
        P("bl", "ta", None),
        P("bl", "ta", None),
        P("bl"),
        P("bl", None),
        P(("bl", "ta"), None),
        P(),
        P(),
        P(),
    )
    out_specs = (P(None, None, "ta", None), P(None, ("bl", "ta"), None, None))
    return jax.shard_map(
        on_device, mesh=mesh, in_specs=in_specs, out_specs=out_specs, check_vma=False
    )
```

```python
import jax
import jax.numpy as jnp
from jax import lax
from jax.experimental import pallas as pl
from jax.experimental.pallas import tpu as pltpu
from jax.sharding import PartitionSpec as P

ANTENNA_COUNT = 350
NGRP = 224
TILE = 128
REACH = 3
HIGH = lax.Precision.HIGHEST
F32 = jnp.float32
BF16 = jnp.bfloat16
I16 = jnp.int16
I32 = jnp.int32
MESH = pl.DeviceIdType.MESH

NX, NZ = 4, 8
NBL = NX * NZ
ROWS = 256
OWN = 48
APAD = 384
A8 = 352
PA = 16
PB = OWN - PA


def nt(a, b, precision=None):
    return lax.dot_general(
        a, b, (((1,), (1,)), ((), ())), preferred_element_type=F32, precision=precision
    )


def power_of_two(k):
    magnitude = jnp.abs(k)
    up = k > 0
    result = jnp.ones(k.shape, F32)
    for bit in (64, 32, 16, 8, 4, 2, 1):
        factor = jnp.where(up, F32(2.0**bit), F32(2.0**-bit))
        result = jnp.where((magnitude & bit) != 0, result * factor, result)
    return result


def encode(g):
    peak = jnp.max(jnp.abs(g), axis=1, keepdims=True)
    k = jnp.floor(jnp.log2(jnp.maximum(peak, F32(2.0**-100)))).astype(I32) + 2
    coded = jnp.round(g * power_of_two(15 - k)).astype(I32)
    lane = lax.broadcasted_iota(I32, g.shape, 1)
    return jnp.where(lane == ANTENNA_COUNT, k, coded)


def solve_kernel(
    blocks, index, inverse, out_a, out_b,
    got, got_index, inv, zg, zp, zm, cp, cm,
    index_send, index_recv, data_send, data_recv,
    a1_send, a1_recv, a2_send, a2_recv, b1_send, b1_recv, b2_send, b2_recv, b3_send, b3_recv,
):
    me = lax.axis_index("bl")
    mx, mz = me // NZ, lax.rem(me, NZ)

    def device(dx, dz):
        return lax.rem(mx + dx + NX, NX) * NZ + lax.rem(mz + dz + NZ, NZ)

    def peer_of(j):
        dz = lax.rem(3 * j, NZ)
        dx = j // NZ
        return device(dx, dz)

    def remote(src, dst, send, recv, peer):
        return pltpu.make_async_remote_copy(
            src_ref=src, dst_ref=dst, send_sem=send, recv_sem=recv,
            device_id={"bl": peer}, device_id_type=MESH,
        )

    barrier = pltpu.get_barrier_semaphore()

    @pl.loop(1, NBL)
    def _(j):
        pl.semaphore_signal(barrier, inc=1, device_id={"bl": peer_of(j)}, device_id_type=MESH)

    pl.semaphore_wait(barrier, NBL - 1)

    def index_copy(j):
        return remote(index, got_index.at[j], index_send.at[j], index_recv.at[j], peer_of(j))

    def data_copy(j):
        peer = peer_of(j)
        return remote(blocks.at[peer], got.at[j], data_send.at[j], data_recv.at[j], peer)

    @pl.loop(1, NBL)
    def _(j):
        index_copy(j).start()

    @pl.loop(1, NBL)
    def _(j):
        data_copy(j).start()

    got[0] = blocks[me]
    got_index[0] = index[...]
    inv[...] = jnp.zeros_like(inv)
    inv[0, 0:ANTENNA_COUNT, 0:ANTENNA_COUNT] = inverse[0]
    inv[1, 0:ANTENNA_COUNT, 0:ANTENNA_COUNT] = inverse[1]
    for ref in (zg, zp, zm, cp, cm):
        ref[...] = jnp.zeros_like(ref)

    @pl.loop(0, NBL)
    def _(j):
        @pl.when(j > 0)
        def _():
            index_copy(j).wait_recv()
            data_copy(j).wait_recv()

        d = got[j]
        ix = got_index[j]

        def row(k):
            return jnp.concatenate([ix[2 * k:2 * k + 1], ix[2 * k + 1:2 * k + 2]], axis=1)

        def hot(k, n):
            return (lax.broadcasted_iota(I32, (n, ROWS), 0) == row(k)).astype(F32)

        group = hot(0, NGRP).astype(BF16)
        first, second = hot(1, A8), hot(2, A8)
        plus = (first + second).astype(BF16)
        minus = (first - second).astype(BF16)
        ones = jnp.ones((16, ROWS), BF16)
        zg[...] += nt(group, jnp.concatenate([d, ones], axis=0))
        zp[...] += nt(plus, d[0:OWN])
        zm[...] += nt(minus, d[OWN:2 * OWN])
        cp[...] += nt(plus, group)
        cm[...] += nt(minus, group)

    sums = zg[...]
    mean = sums[:, 0:2 * OWN] / sums[:, 2 * OWN:2 * OWN + 1]
    for s, (z, c) in enumerate(((zp, cp), (zm, cm))):
        rhs = z[...] - jnp.dot(
            c[...], mean[:, s * OWN:(s + 1) * OWN], precision=HIGH, preferred_element_type=F32
        )
        g = nt(rhs.T, inv[s], HIGH)
        coded = encode(g).astype(I16)
        out_a[mz, mx, :, s * APAD:(s + 1) * APAD] = coded[0:PA]
        out_b[mx, mz, :, s * APAD:(s + 1) * APAD] = coded[PA:OWN]

    def x_of(dx):
        return lax.rem(mx + dx + NX, NX)

    def z_of(dz):
        return lax.rem(mz + dz + NZ, NZ)

    started = []

    def begin(copy):
        copy.start()
        started.append(copy)

    def a1(dx, src_x):
        slot = out_a.at[mz, src_x]
        return remote(slot, slot, a1_send.at[dx], a1_recv.at[dx], device(dx, 0))

    def a2(direction, hop, src_z):
        slot = out_a.at[src_z]
        if hop == 4:
            slot = slot.at[pl.ds(2 * direction, 2)]
        return remote(
            slot, slot, a2_send.at[direction, hop - 1], a2_recv.at[direction, hop - 1],
            device(0, 1 - 2 * direction),
        )

    def b1(direction, hop, src_z):
        slot = out_b.at[mx, src_z]
        if hop == 4:
            slot = slot.at[pl.ds(16 * direction, 16)]
        return remote(
            slot, slot, b1_send.at[direction, hop - 1], b1_recv.at[direction, hop - 1],
            device(0, 1 - 2 * direction),
        )

    def b2(direction, dz, src_x):
        slot = out_b.at[src_x, z_of(dz)]
        n = dz % NZ
        return remote(
            slot, slot, b2_send.at[direction, n], b2_recv.at[direction, n],
            device(1 - 2 * direction, 0),
        )

    def b3(direction, dz, src_x):
        slot = out_b.at[src_x, z_of(dz)]
        n = dz % NZ
        return remote(slot, slot, b3_send.at[n], b3_recv.at[n], device(1 - 2 * direction, 0))

    for direction in (0, 1):
        begin(b1(direction, 1, mz))
    for dx in (1, 3, 2):
        begin(a1(dx, mx))
    for direction in (0, 1):
        begin(b2(direction, 0, mx))
    for dx in (1, 3, 2):
        a1(dx, x_of(-dx)).wait_recv()
    for direction in (0, 1):
        begin(a2(direction, 1, mz))
    for hop in (1, 2, 3, 4):
        for direction in (0, 1):
            dz = -hop if direction == 0 else hop
            b1(direction, hop, z_of(dz)).wait_recv()
            if hop < 4:
                begin(b1(direction, hop + 1, z_of(dz)))
                for way in (0, 1):
                    begin(b2(way, dz, mx))
        if hop == 4:
            for way in (0, 1):
                begin(b2(way, 4, mx))
        for direction in (0, 1):
            dz = -hop if direction == 0 else hop
            a2(direction, hop, z_of(dz)).wait_recv()
            if hop < 4:
                begin(a2(direction, hop + 1, z_of(dz)))
    order = (0, -1, 1, -2, 2, -3, 3, 4)
    for i, dz in enumerate(order):
        for way in (0, 1):
            source = x_of(-1 if way == 0 else 1)
            b2(way, dz, source).wait_recv()
            if i % 2 == way:
                begin(b3(way, dz, source))
    for i, dz in enumerate(order):
        b3(i % 2, dz, x_of(2)).wait_recv()
    for copy in started:
        copy.wait_send()

    @pl.loop(1, NBL)
    def _(j):
        index_copy(j).wait_send()
        data_copy(j).wait_send()


def solve_gains(blocks, index, inverse):
    dma = pltpu.SemaphoreType.DMA
    vmem = pl.BlockSpec(memory_space=pltpu.VMEM)
    return pl.pallas_call(
        solve_kernel,
        name="solve_gains",
        out_shape=(
            jax.ShapeDtypeStruct((NZ, NX, PA, 2 * APAD), I16),
            jax.ShapeDtypeStruct((NX, NZ, PB, 2 * APAD), I16),
        ),
        in_specs=[vmem] * 3,
        out_specs=(vmem, vmem),
        scratch_shapes=[
            pltpu.VMEM((NBL, 2 * OWN, ROWS), BF16),
            pltpu.VMEM((NBL, 8, 128), I32),
            pltpu.VMEM((2, APAD, A8), F32),
            pltpu.VMEM((NGRP, 2 * OWN + 16), F32),
            pltpu.VMEM((A8, OWN), F32),
            pltpu.VMEM((A8, OWN), F32),
            pltpu.VMEM((A8, NGRP), F32),
            pltpu.VMEM((A8, NGRP), F32),
            dma((NBL,)), dma((NBL,)), dma((NBL,)), dma((NBL,)),
            dma((NX,)), dma((NX,)),
            dma((2, 4)), dma((2, 4)), dma((2, 4)), dma((2, 4)),
            dma((2, NZ)), dma((2, NZ)), dma((NZ,)), dma((NZ,)),
        ],
        compiler_params=pltpu.CompilerParams(
            collective_id=0, has_side_effects=True, vmem_limit_bytes=48 * 2**20
        ),
    )(blocks, index, inverse)


def mix_channels(values, channel_kernel):
    leading = values.shape[:-1]
    tile_count = values.shape[-1] // TILE
    tiled = values.reshape(leading + (tile_count, TILE))
    pad_spec = [(0, 0)] * len(leading) + [(REACH, REACH), (0, 0)]
    padded = jnp.pad(tiled, pad_spec)
    summed = jnp.zeros(leading + (tile_count, TILE), jnp.float32)
    for offset in range(2 * REACH + 1):
        window = lax.slice_in_dim(padded, offset, offset + tile_count, axis=len(leading))
        summed = summed + jnp.einsum(
            "...kj,ij->...ki", window, channel_kernel[offset], preferred_element_type=jnp.float32
        )
    return summed.reshape(leading + (tile_count * TILE,))


def fill_block(calibrated, tile_flag_mask, integration_kernel, channel_kernel):
    weight = jnp.repeat((1 - tile_flag_mask).astype(jnp.bfloat16), TILE, axis=1)
    masked = calibrated * weight[None, :, None, :]
    mixed = mix_channels(masked, channel_kernel)
    numerator = jnp.einsum("tu,kbuf->kbtf", integration_kernel, mixed, precision=HIGH)
    weight_mix = mix_channels(weight, channel_kernel)
    denominator = jnp.sum(integration_kernel, axis=1)[None, :, None] * weight_mix[:, None, :]
    keep = weight.astype(jnp.float32)[None, :, None, :]
    return keep * calibrated.astype(jnp.float32) + (1.0 - keep) * numerator / denominator[None]


def decode(out_a, out_b):
    coded = jnp.concatenate(
        [out_a.transpose(1, 0, 2, 3), out_b], axis=2
    ).reshape(NBL * OWN, 2, APAD)
    scale = power_of_two(coded[:, :, ANTENNA_COUNT:ANTENNA_COUNT + 1].astype(I32) - 15)
    return coded[:, :, :ANTENNA_COUNT].astype(F32) * scale


def on_device(
    log_amplitude,
    phase,
    redundant_group_index,
    antenna_couples,
    tile_flag_mask,
    inverse,
    integration_kernel,
    channel_kernel,
):
    data = jnp.stack([log_amplitude[:, 0], phase[:, 0]])
    blocks = data.reshape(2, ROWS, NBL, OWN).transpose(2, 0, 3, 1).reshape(NBL, 2 * OWN, ROWS)
    index = jnp.concatenate([redundant_group_index[None, :], antenna_couples.T], axis=0)
    index = jnp.pad(index.reshape(6, 128), ((0, 2), (0, 0)))
    gains = decode(*solve_gains(blocks, index, inverse))
    antenna_gains = gains.transpose(1, 2, 0)

    first_local = antenna_couples[:, 0]
    second_local = antenna_couples[:, 1]
    amp, ph = antenna_gains[0], antenna_gains[1]
    u = data[0].astype(jnp.float32) - amp[first_local] - amp[second_local]
    v = data[1].astype(jnp.float32) - ph[first_local] + ph[second_local]
    magnitude = jnp.exp(u)
    calibrated = jnp.stack([magnitude * jnp.cos(v), magnitude * jnp.sin(v)]).astype(jnp.bfloat16)
    filled = fill_block(
        lax.all_to_all(calibrated[:, :, None], "ta", split_axis=1, concat_axis=2, tiled=True),
        tile_flag_mask,
        integration_kernel,
        channel_kernel,
    )
    return (antenna_gains[:, :, None], filled)


def solution(mesh):
    in_specs = (
        P("bl", "ta", None),
        P("bl", "ta", None),
        P("bl"),
        P("bl", None),
        P(("bl", "ta"), None),
        P(),
        P(),
        P(),
    )
    out_specs = (P(None, None, "ta", None), P(None, ("bl", "ta"), None, None))
    return jax.shard_map(
        on_device, mesh=mesh, in_specs=in_specs, out_specs=out_specs, check_vma=False
    )
```

```python
import jax
import jax.numpy as jnp
from jax import lax
from jax.experimental import pallas as pl
from jax.experimental.pallas import tpu as pltpu
from jax.sharding import PartitionSpec as P

ANTENNA_COUNT = 350
NGRP = 224
TILE = 128
REACH = 3
HIGH = lax.Precision.HIGHEST
F32 = jnp.float32
BF16 = jnp.bfloat16
I16 = jnp.int16
I32 = jnp.int32
MESH = pl.DeviceIdType.MESH

NX, NZ = 4, 8
NBL = NX * NZ
ROWS = 256
OWN = 48
APAD = 384
A8 = 352
PA = 16
PB = OWN - PA


def nt(a, b, precision=None):
    return lax.dot_general(
        a, b, (((1,), (1,)), ((), ())), preferred_element_type=F32, precision=precision
    )


def encode(g):
    peak = jnp.max(jnp.abs(g), axis=1, keepdims=True)
    k = jnp.floor(jnp.log2(jnp.maximum(peak, F32(2.0**-100)))).astype(I32) + 2
    coded = jnp.round(g * jnp.exp2((15 - k).astype(F32))).astype(I32)
    lane = lax.broadcasted_iota(I32, g.shape, 1)
    return jnp.where(lane == ANTENNA_COUNT, k, coded)


def solve_kernel(
    blocks, index, inverse, out_a, out_b,
    got, got_index, inv, zg, zp, zm, cp, cm,
    index_send, index_recv, data_send, data_recv,
    a1_send, a1_recv, a2_send, a2_recv, b1_send, b1_recv, b2_send, b2_recv, b3_send, b3_recv,
):
    me = lax.axis_index("bl")
    mx, mz = me // NZ, lax.rem(me, NZ)

    def device(dx, dz):
        return lax.rem(mx + dx + NX, NX) * NZ + lax.rem(mz + dz + NZ, NZ)

    def peer_of(j):
        dz = lax.rem(3 * j, NZ)
        dx = j // NZ
        return device(dx, dz)

    def remote(src, dst, send, recv, peer):
        return pltpu.make_async_remote_copy(
            src_ref=src, dst_ref=dst, send_sem=send, recv_sem=recv,
            device_id={"bl": peer}, device_id_type=MESH,
        )

    barrier = pltpu.get_barrier_semaphore()

    @pl.loop(1, NBL)
    def _(j):
        pl.semaphore_signal(barrier, inc=1, device_id={"bl": peer_of(j)}, device_id_type=MESH)

    pl.semaphore_wait(barrier, NBL - 1)

    def index_copy(j):
        return remote(index, got_index.at[j], index_send.at[j], index_recv.at[j], peer_of(j))

    def data_copy(j):
        peer = peer_of(j)
        return remote(blocks.at[peer], got.at[j], data_send.at[j], data_recv.at[j], peer)

    @pl.loop(1, NBL)
    def _(j):
        index_copy(j).start()

    @pl.loop(1, NBL)
    def _(j):
        data_copy(j).start()

    got[0] = blocks[me]
    got_index[0] = index[...]
    inv[...] = jnp.zeros_like(inv)
    inv[0, 0:ANTENNA_COUNT, 0:ANTENNA_COUNT] = inverse[0]
    inv[1, 0:ANTENNA_COUNT, 0:ANTENNA_COUNT] = inverse[1]
    for ref in (zg, zp, zm, cp, cm):
        ref[...] = jnp.zeros_like(ref)

    @pl.loop(0, NBL)
    def _(j):
        @pl.when(j > 0)
        def _():
            index_copy(j).wait_recv()
            data_copy(j).wait_recv()

        d = got[j]
        ix = got_index[j]

        def row(k):
            return jnp.concatenate([ix[2 * k:2 * k + 1], ix[2 * k + 1:2 * k + 2]], axis=1)

        def hot(k, n):
            return (lax.broadcasted_iota(I32, (n, ROWS), 0) == row(k)).astype(F32)

        group = hot(0, NGRP).astype(BF16)
        first, second = hot(1, A8), hot(2, A8)
        plus = (first + second).astype(BF16)
        minus = (first - second).astype(BF16)
        ones = jnp.ones((16, ROWS), BF16)
        zg[...] += nt(group, jnp.concatenate([d, ones], axis=0))
        zp[...] += nt(plus, d[0:OWN])
        zm[...] += nt(minus, d[OWN:2 * OWN])
        cp[...] += nt(plus, group)
        cm[...] += nt(minus, group)

    sums = zg[...]
    mean = sums[:, 0:2 * OWN] / sums[:, 2 * OWN:2 * OWN + 1]
    for s, (z, c) in enumerate(((zp, cp), (zm, cm))):
        rhs = z[...] - jnp.dot(
            c[...], mean[:, s * OWN:(s + 1) * OWN], precision=HIGH, preferred_element_type=F32
        )
        g = nt(rhs.T, inv[s], HIGH)
        coded = encode(g).astype(I16)
        out_a[mz, mx, :, s * APAD:(s + 1) * APAD] = coded[0:PA]
        out_b[mx, mz, :, s * APAD:(s + 1) * APAD] = coded[PA:OWN]

    def x_of(dx):
        return lax.rem(mx + dx + NX, NX)

    def z_of(dz):
        return lax.rem(mz + dz + NZ, NZ)

    started = []

    def begin(copy):
        copy.start()
        started.append(copy)

    def a1(dx, src_x):
        slot = out_a.at[mz, src_x]
        return remote(slot, slot, a1_send.at[dx], a1_recv.at[dx], device(dx, 0))

    def a2(direction, hop, src_z):
        slot = out_a.at[src_z]
        if hop == 4:
            slot = slot.at[pl.ds(2 * direction, 2)]
        return remote(
            slot, slot, a2_send.at[direction, hop - 1], a2_recv.at[direction, hop - 1],
            device(0, 1 - 2 * direction),
        )

    def b1(direction, hop, src_z):
        slot = out_b.at[mx, src_z]
        if hop == 4:
            slot = slot.at[pl.ds(16 * direction, 16)]
        return remote(
            slot, slot, b1_send.at[direction, hop - 1], b1_recv.at[direction, hop - 1],
            device(0, 1 - 2 * direction),
        )

    def b2(direction, dz, src_x):
        slot = out_b.at[src_x, z_of(dz)]
        n = dz % NZ
        return remote(
            slot, slot, b2_send.at[direction, n], b2_recv.at[direction, n],
            device(1 - 2 * direction, 0),
        )

    def b3(direction, dz, src_x):
        slot = out_b.at[src_x, z_of(dz)]
        n = dz % NZ
        return remote(slot, slot, b3_send.at[n], b3_recv.at[n], device(1 - 2 * direction, 0))

    for direction in (0, 1):
        begin(b1(direction, 1, mz))
    for dx in (1, 3, 2):
        begin(a1(dx, mx))
    for direction in (0, 1):
        begin(b2(direction, 0, mx))
    for dx in (1, 3, 2):
        a1(dx, x_of(-dx)).wait_recv()
    for direction in (0, 1):
        begin(a2(direction, 1, mz))
    for hop in (1, 2, 3, 4):
        for direction in (0, 1):
            dz = -hop if direction == 0 else hop
            b1(direction, hop, z_of(dz)).wait_recv()
            if hop < 4:
                begin(b1(direction, hop + 1, z_of(dz)))
                for way in (0, 1):
                    begin(b2(way, dz, mx))
        if hop == 4:
            for way in (0, 1):
                begin(b2(way, 4, mx))
        for direction in (0, 1):
            dz = -hop if direction == 0 else hop
            a2(direction, hop, z_of(dz)).wait_recv()
            if hop < 4:
                begin(a2(direction, hop + 1, z_of(dz)))
    order = (0, -1, 1, -2, 2, -3, 3, 4)
    for i, dz in enumerate(order):
        for way in (0, 1):
            source = x_of(-1 if way == 0 else 1)
            b2(way, dz, source).wait_recv()
            if i % 2 == way:
                begin(b3(way, dz, source))
    for i, dz in enumerate(order):
        b3(i % 2, dz, x_of(2)).wait_recv()
    for copy in started:
        copy.wait_send()

    @pl.loop(1, NBL)
    def _(j):
        index_copy(j).wait_send()
        data_copy(j).wait_send()


def solve_gains(blocks, index, inverse):
    dma = pltpu.SemaphoreType.DMA
    vmem = pl.BlockSpec(memory_space=pltpu.VMEM)
    return pl.pallas_call(
        solve_kernel,
        name="solve_gains",
        out_shape=(
            jax.ShapeDtypeStruct((NZ, NX, PA, 2 * APAD), I16),
            jax.ShapeDtypeStruct((NX, NZ, PB, 2 * APAD), I16),
        ),
        in_specs=[vmem] * 3,
        out_specs=(vmem, vmem),
        scratch_shapes=[
            pltpu.VMEM((NBL, 2 * OWN, ROWS), BF16),
            pltpu.VMEM((NBL, 8, 128), I32),
            pltpu.VMEM((2, APAD, A8), F32),
            pltpu.VMEM((NGRP, 2 * OWN + 16), F32),
            pltpu.VMEM((A8, OWN), F32),
            pltpu.VMEM((A8, OWN), F32),
            pltpu.VMEM((A8, NGRP), F32),
            pltpu.VMEM((A8, NGRP), F32),
            dma((NBL,)), dma((NBL,)), dma((NBL,)), dma((NBL,)),
            dma((NX,)), dma((NX,)),
            dma((2, 4)), dma((2, 4)), dma((2, 4)), dma((2, 4)),
            dma((2, NZ)), dma((2, NZ)), dma((NZ,)), dma((NZ,)),
        ],
        compiler_params=pltpu.CompilerParams(
            collective_id=0, has_side_effects=True, vmem_limit_bytes=48 * 2**20
        ),
    )(blocks, index, inverse)


NTA = 8
NT = 8
BASE = ROWS // NTA
CH = NBL * OWN
PARTS = 3
CW = CH // PARTS
NTILE = CH // TILE
PAIRS = NTILE // 2


def sin_cos(v):
    n = jnp.round(v * F32(0.6366197723675814))
    r = v - n * F32(1.5703125)
    r = r - n * F32(4.837512969970703125e-4)
    r = r - n * F32(7.54978995489188216e-8)
    quadrant = n.astype(I32)
    z = r * r
    s = ((F32(-1.9515295891e-4) * z + F32(8.3321608736e-3)) * z - F32(1.6666654611e-1)) * z * r + r
    c = (
        (F32(2.443315711809948e-5) * z - F32(1.388731625493765e-3)) * z + F32(4.166664568298827e-2)
    ) * z * z - F32(0.5) * z + F32(1.0)
    swap = (quadrant & 1) != 0
    sine = jnp.where(swap, c, s)
    cosine = jnp.where(swap, s, c)
    sine = jnp.where((quadrant & 2) != 0, -sine, sine)
    cosine = jnp.where(((quadrant + 1) & 2) != 0, -cosine, cosine)
    return sine, cosine


def fill_kernel(
    coded_a, coded_b, amp, ph, couples, flags, times, channel, gains, filled,
    g_full, g_high, g_low, select, combo, wide_kernel, keep, keep_wide, masked, rden, mixed,
    out_cal, in_cal, send_sem, recv_sem,
):
    me = lax.axis_index("ta")
    barrier = pltpu.get_barrier_semaphore()

    def peer_of(j):
        return lax.rem(me + j, NTA)

    @pl.loop(1, NTA)
    def _(j):
        pl.semaphore_signal(barrier, inc=1, device_id={"ta": peer_of(j)}, device_id_type=MESH)

    @pl.loop(0, NBL)
    def _(i):
        x, z = i // NZ, lax.rem(i, NZ)
        start = pl.multiple_of(i * OWN, 16)
        for coded, first, size in ((coded_a[z, x], 0, PA), (coded_b[x, z], PA, PB)):
            q = coded.astype(I32)
            rows = pl.ds(start + first, size)
            for s in (0, 1):
                part = q[:, s * APAD:(s + 1) * APAD]
                k = part[:, ANTENNA_COUNT:ANTENNA_COUNT + 1] - 15
                g = part.astype(F32) * jnp.exp2(k.astype(F32))
                high = g.astype(BF16)
                cols = slice(s * APAD, (s + 1) * APAD)
                g_full[rows, cols] = g
                g_high[rows, cols] = high
                g_low[rows, cols] = (g - high.astype(F32)).astype(BF16)

    label = lax.broadcasted_iota(I32, (ROWS, APAD), 1)
    first = (couples[:, 0:1] == label).astype(F32)
    second = (couples[:, 1:2] == label).astype(F32)
    select[0] = (first + second).astype(BF16)
    select[1] = (first - second).astype(BF16)

    def copy_out(j, n):
        return pltpu.make_async_remote_copy(
            src_ref=out_cal.at[n, peer_of(j)], dst_ref=in_cal.at[j, n],
            send_sem=send_sem.at[j, n], recv_sem=recv_sem.at[j, n],
            device_id={"ta": peer_of(j)}, device_id_type=MESH,
        )

    for n in range(PARTS):
        cols = slice(n * CW, (n + 1) * CW)
        for s in (0, 1):
            lanes = slice(s * APAD, (s + 1) * APAD)
            combo[s] = nt(select[s], g_high[cols, lanes]) + nt(select[s], g_low[cols, lanes])

        @pl.loop(0, NTA)
        def _(d):
            rows = pl.ds(pl.multiple_of(d * BASE, BASE), BASE)
            u = amp[rows, cols].astype(F32) - combo[0, rows, :]
            v = ph[rows, cols].astype(F32) - combo[1, rows, :]
            magnitude = jnp.exp(u)
            sine, cosine = sin_cos(v)
            out_cal[n, d, 0] = (magnitude * cosine).astype(BF16)
            out_cal[n, d, 1] = (magnitude * sine).astype(BF16)

        if n == 0:
            pl.semaphore_wait(barrier, NTA - 1)

        @pl.loop(1, NTA)
        def _(j):
            copy_out(j, n).start()

        in_cal[0, n] = out_cal[n, me]

    wide_kernel[...] = jnp.zeros_like(wide_kernel)
    for c in (0, 1):
        for o in range(2 * REACH + 1):
            wide_kernel[c * TILE:(c + 1) * TILE, (c + o) * TILE:(c + o + 1) * TILE] = channel[o]
    masked[...] = jnp.zeros_like(masked)
    keep_wide[...] = jnp.zeros_like(keep_wide)
    for k in range(NTILE):
        w = jnp.broadcast_to(1.0 - flags[:, k:k + 1].astype(F32), (BASE, TILE))
        keep[:, k * TILE:(k + 1) * TILE] = w
        keep_wide[:, (k + REACH) * TILE:(k + REACH + 1) * TILE] = w.astype(BF16)
    for p in range(PAIRS):
        window = slice(2 * TILE * p, 2 * TILE * p + 8 * TILE)
        rden[:, 2 * TILE * p:2 * TILE * (p + 1)] = 1.0 / nt(keep_wide[:, window], wide_kernel[...])
    mixed[...] = jnp.zeros_like(mixed)

    for s in (0, 1):
        @pl.loop(0, NTILE)
        def _(k):
            block = g_full[pl.ds(pl.multiple_of(k * TILE, TILE), TILE), s * APAD:(s + 1) * APAD]
            gains[pl.ds(s * ANTENNA_COUNT * NTILE + k, ANTENNA_COUNT, stride=NTILE), :] = (
                block.T[0:ANTENNA_COUNT]
            )

    @pl.loop(0, NTA)
    def _(j):
        @pl.when(j > 0)
        def _():
            for n in range(PARTS):
                copy_out(j, n).wait_recv()

        t = lax.rem(me - j + NTA, NTA)
        for n in range(PARTS):
            w = keep[:, n * CW:(n + 1) * CW].astype(BF16)
            for c in (0, 1):
                masked[c * BASE:(c + 1) * BASE, REACH * TILE + n * CW:REACH * TILE + (n + 1) * CW] = (
                    in_cal[j, n, c] * w
                )
        for p in range(PAIRS):
            window = slice(2 * TILE * p, 2 * TILE * p + 8 * TILE)
            mix = nt(masked[:, window], wide_kernel[...])
            for to in range(NT):
                mixed[to, :, 2 * TILE * p:2 * TILE * (p + 1)] += times[to, t] * mix

    @pl.loop(0, NT)
    def _(to):
        j = lax.rem(me - to + NTA, NTA)
        total = times[to, 0]
        for t in range(1, NT):
            total = total + times[to, t]
        scale = 1.0 / jnp.full((1, CW), total, F32)
        for n in range(PARTS):
            cols = slice(n * CW, (n + 1) * CW)
            w = keep[:, cols]
            ratio = rden[:, cols] * scale
            for c in (0, 1):
                value = jnp.where(
                    w > 0.5, in_cal[j, n, c].astype(F32),
                    mixed[to, c * BASE:(c + 1) * BASE, cols] * ratio,
                )
                for i in range(CW // TILE):
                    k = n * (CW // TILE) + i
                    start = c * BASE * NTILE * NT + k * NT + to
                    filled[pl.ds(start, BASE, stride=NTILE * NT), :] = (
                        value[:, i * TILE:(i + 1) * TILE]
                    )

    @pl.loop(1, NTA)
    def _(j):
        for n in range(PARTS):
            copy_out(j, n).wait_send()


def calibrate_and_fill(coded_a, coded_b, amp, ph, couples, flags, times, channel):
    dma = pltpu.SemaphoreType.DMA
    vmem = pl.BlockSpec(memory_space=pltpu.VMEM)
    smem = pl.BlockSpec(memory_space=pltpu.SMEM)
    return pl.pallas_call(
        fill_kernel,
        name="calibrate_and_fill",
        out_shape=(
            jax.ShapeDtypeStruct((2 * ANTENNA_COUNT * NTILE, TILE), F32),
            jax.ShapeDtypeStruct((2 * BASE * NTILE * NT, TILE), F32),
        ),
        in_specs=[vmem] * 6 + [smem, vmem],
        out_specs=(vmem, vmem),
        scratch_shapes=[
            pltpu.VMEM((CH, 2 * APAD), F32),
            pltpu.VMEM((CH, 2 * APAD), BF16),
            pltpu.VMEM((CH, 2 * APAD), BF16),
            pltpu.VMEM((2, ROWS, APAD), BF16),
            pltpu.VMEM((2, ROWS, CW), F32),
            pltpu.VMEM((2 * TILE, 8 * TILE), BF16),
            pltpu.VMEM((BASE, CH), F32),
            pltpu.VMEM((BASE, CH + 6 * TILE), BF16),
            pltpu.VMEM((2 * BASE, CH + 6 * TILE), BF16),
            pltpu.VMEM((BASE, CH), F32),
            pltpu.VMEM((NT, 2 * BASE, CH), F32),
            pltpu.VMEM((PARTS, NTA, 2, BASE, CW), BF16),
            pltpu.VMEM((NTA, PARTS, 2, BASE, CW), BF16),
            dma((NTA, PARTS)), dma((NTA, PARTS)),
        ],
        compiler_params=pltpu.CompilerParams(
            collective_id=1, has_side_effects=True, vmem_limit_bytes=50 * 2**20
        ),
    )(coded_a, coded_b, amp, ph, couples, flags, times, channel)


def on_device(
    log_amplitude,
    phase,
    redundant_group_index,
    antenna_couples,
    tile_flag_mask,
    inverse,
    integration_kernel,
    channel_kernel,
):
    amp, ph = log_amplitude[:, 0], phase[:, 0]
    data = jnp.stack([amp, ph])
    blocks = data.reshape(2, ROWS, NBL, OWN).transpose(2, 0, 3, 1).reshape(NBL, 2 * OWN, ROWS)
    index = jnp.concatenate([redundant_group_index[None, :], antenna_couples.T], axis=0)
    index = jnp.pad(index.reshape(6, 128), ((0, 2), (0, 0)))
    coded_a, coded_b = solve_gains(blocks, index, inverse)
    gains, filled = calibrate_and_fill(
        coded_a, coded_b, amp, ph, antenna_couples, tile_flag_mask, integration_kernel,
        channel_kernel,
    )
    return (
        gains.reshape(2, ANTENNA_COUNT, 1, CH),
        filled.reshape(2, BASE, NTILE, NT, TILE).transpose(0, 1, 3, 2, 4).reshape(2, BASE, NT, CH),
    )


def solution(mesh):
    in_specs = (
        P("bl", "ta", None),
        P("bl", "ta", None),
        P("bl"),
        P("bl", None),
        P(("bl", "ta"), None),
        P(),
        P(),
        P(),
    )
    out_specs = (P(None, None, "ta", None), P(None, ("bl", "ta"), None, None))
    return jax.shard_map(
        on_device, mesh=mesh, in_specs=in_specs, out_specs=out_specs, check_vma=False
    )
```

```python
import jax
import jax.numpy as jnp
from jax import lax
from jax.experimental import pallas as pl
from jax.experimental.pallas import tpu as pltpu
from jax.sharding import PartitionSpec as P

ANTENNA_COUNT = 350
NGRP = 224
TILE = 128
REACH = 3
HIGH = lax.Precision.HIGHEST
F32 = jnp.float32
BF16 = jnp.bfloat16
I16 = jnp.int16
I32 = jnp.int32
MESH = pl.DeviceIdType.MESH

NX, NZ = 4, 8
NBL = NX * NZ
NTA = 8
NT = 8
ROWS = 256
BASE = ROWS // NTA
CH = 1536
PARTS = 3
CW = CH // PARTS
OWN = CW // NBL
APAD = 384
A8 = 352
HOT = NGRP + 2 * A8
NTILE = CH // TILE
PAIR = 2 * TILE
WINDOW = 8 * TILE
EDGE = REACH * TILE
LINE = 2 * BASE


def nt(a, b, precision=None):
    return lax.dot_general(
        a, b, (((1,), (1,)), ((), ())), preferred_element_type=F32, precision=precision
    )


def encode(g):
    peak = jnp.max(jnp.abs(g), axis=1, keepdims=True)
    k = jnp.floor(jnp.log2(jnp.maximum(peak, F32(2.0**-100)))).astype(I32) + 2
    coded = jnp.round(g * jnp.exp2((15 - k).astype(F32))).astype(I32)
    lane = lax.broadcasted_iota(I32, g.shape, 1)
    return jnp.where(lane == ANTENNA_COUNT, k, coded)


def sin_cos(v):
    n = jnp.round(v * F32(0.6366197723675814))
    r = v - n * F32(1.5703125)
    r = r - n * F32(4.837512969970703125e-4)
    r = r - n * F32(7.54978995489188216e-8)
    quadrant = n.astype(I32)
    z = r * r
    s = ((F32(-1.9515295891e-4) * z + F32(8.3321608736e-3)) * z - F32(1.6666654611e-1)) * z * r + r
    c = (
        (F32(2.443315711809948e-5) * z - F32(1.388731625493765e-3)) * z + F32(4.166664568298827e-2)
    ) * z * z - F32(0.5) * z + F32(1.0)
    swap = (quadrant & 1) != 0
    sine = jnp.where(swap, c, s)
    cosine = jnp.where(swap, s, c)
    sine = jnp.where((quadrant & 2) != 0, -sine, sine)
    cosine = jnp.where(((quadrant + 1) & 2) != 0, -cosine, cosine)
    return sine, cosine


def whole_kernel(
    amp, ph, group_row, couples, flags, times, channel, inverse, gains, filled,
    send, got, index, got_index, hot, inv, total, sums, count, shared,
    g_full, g_high, g_low, select, combo, wide, keep, keep_wide, masked, rden, mixed,
    out_cal, in_cal,
    index_send, index_recv, data_send, data_recv, b1_send, b1_recv, b2_send, b2_recv,
    b3_send, b3_recv, cal_send, cal_recv,
):
    me = lax.axis_index("bl")
    mx, mz = me // NZ, lax.rem(me, NZ)
    mt = lax.axis_index("ta")

    def x_of(dx):
        return lax.rem(mx + dx + NX, NX)

    def z_of(dz):
        return lax.rem(mz + dz + NZ, NZ)

    def device(dx, dz):
        return x_of(dx) * NZ + z_of(dz)

    def peer_of(j):
        return device(j // NZ, lax.rem(3 * j, NZ))

    def time_peer(j):
        return lax.rem(mt + j, NTA)

    def remote(src, dst, send_sem, recv_sem, axis, peer):
        return pltpu.make_async_remote_copy(
            src_ref=src, dst_ref=dst, send_sem=send_sem, recv_sem=recv_sem,
            device_id={axis: peer}, device_id_type=MESH,
        )

    def index_copy(j):
        return remote(
            index, got_index.at[j], index_send.at[j], index_recv.at[j], "bl", peer_of(j)
        )

    def data_copy(n, j):
        peer = peer_of(j)
        return remote(
            send.at[n, peer], got.at[n, j], data_send.at[n, j], data_recv.at[n, j], "bl", peer
        )

    def cal_copy(n, j):
        peer = time_peer(j)
        return remote(
            out_cal.at[n, peer], in_cal.at[n, j], cal_send.at[n, j], cal_recv.at[n, j], "ta", peer
        )

    def b1(n, dz, step, half=None):
        slot = shared.at[n, mx, z_of(dz)]
        number = (step - dz) % NZ
        if half is not None:
            slot = slot.at[:, pl.ds(half * APAD, APAD)]
            number = 4 * half
        return remote(slot, slot, b1_send.at[n, number], b1_recv.at[n, number], "bl", device(0, step))

    def b1_wait(n, dz, half=None):
        slot = shared.at[n, mx, z_of(dz)]
        number = (-dz) % NZ
        if half is not None:
            slot = slot.at[:, pl.ds(half * APAD, APAD)]
            number = 4 * half
        remote(slot, slot, b1_send.at[n, number], b1_recv.at[n, number], "bl", device(0, 1)).wait_recv()

    def b2(n, way, dz, src_x):
        slot = shared.at[n, src_x, z_of(dz)]
        number = dz % NZ
        return remote(
            slot, slot, b2_send.at[n, way, number], b2_recv.at[n, way, number],
            "bl", device(1 - 2 * way, 0),
        )

    def b3(n, way, dz, src_x):
        slot = shared.at[n, src_x, z_of(dz)]
        number = dz % NZ
        return remote(
            slot, slot, b3_send.at[n, number], b3_recv.at[n, number], "bl", device(1 - 2 * way, 0)
        )

    barrier = pltpu.get_barrier_semaphore()

    @pl.loop(1, NBL)
    def _(j):
        pl.semaphore_signal(barrier, inc=1, device_id={"bl": peer_of(j)}, device_id_type=MESH)

    @pl.loop(1, NTA)
    def _(j):
        pl.semaphore_signal(barrier, inc=1, device_id={"ta": time_peer(j)}, device_id_type=MESH)

    def turn(n):
        cols = slice(n * CW, (n + 1) * CW)
        send[n, :, 0:OWN, :] = amp[:, cols].T.reshape(NBL, OWN, ROWS)
        send[n, :, OWN:2 * OWN, :] = ph[:, cols].T.reshape(NBL, OWN, ROWS)
        got[n, 0] = send[n, me]

    index[...] = jnp.concatenate(
        [
            ref[k:k + 1, h * TILE:(h + 1) * TILE]
            for ref, k in ((group_row, 0), (couples, 0), (couples, 1)) for h in (0, 1)
        ] + [jnp.zeros((2, TILE), I32)], axis=0
    ).astype(I16)
    turn(0)
    pl.semaphore_wait(barrier, NBL - 1 + NTA - 1)

    @pl.loop(1, NBL)
    def _(j):
        index_copy(j).start()

    @pl.loop(1, NBL)
    def _(j):
        data_copy(0, j).start()

    turn(1)
    turn(2)

    got_index[0] = index[...]
    inv[...] = jnp.zeros_like(inv)
    for s in (0, 1):
        inv[s, 0:ANTENNA_COUNT, 0:ANTENNA_COUNT] = inverse[:, s, :]
    label = lax.broadcasted_iota(I32, (APAD, ROWS), 0)
    first = (couples[0:1, :] == label).astype(F32)
    second = (couples[1:2, :] == label).astype(F32)
    select[0] = (first + second).T.astype(BF16)
    select[1] = (first - second).T.astype(BF16)
    wide[...] = jnp.zeros_like(wide)
    for c in (0, 1):
        for o in range(2 * REACH + 1):
            wide[c * TILE:(c + 1) * TILE, (c + o) * TILE:(c + o + 1) * TILE] = channel[o]
    masked[...] = jnp.zeros_like(masked)
    keep_wide[...] = jnp.zeros_like(keep_wide)
    tile = lax.broadcasted_iota(I32, (NTILE, CH), 1) // TILE
    spread = (tile == lax.broadcasted_iota(I32, (NTILE, CH), 0)).astype(F32).astype(BF16)
    open_tiles = (1 - flags[...]).astype(F32).astype(BF16)
    keep[...] = lax.dot_general(
        open_tiles, spread, (((0,), (0,)), ((), ())), preferred_element_type=F32
    )
    keep_wide[:, EDGE:EDGE + CH] = keep[...].astype(BF16)
    for p in range(NTILE // 2):
        rden[:, PAIR * p:PAIR * (p + 1)] = 1.0 / nt(
            keep_wide[:, PAIR * p:PAIR * p + WINDOW], wide[...]
        )

    def clear(*refs):
        for ref in refs:
            ref[...] = jnp.zeros_like(ref)

    clear(total)

    def add_sums(n, low, high):
        @pl.loop(low, high)
        def _(j):
            @pl.when(j > 0)
            def _():
                if n == 0:
                    index_copy(j).wait_recv()
                data_copy(n, j).wait_recv()
                if n + 1 < PARTS:
                    data_copy(n + 1, j).start()

            d = got[n, j]
            if n == 0:
                ix = got_index[j].astype(I32)

                def one_hot(k, size):
                    row = jnp.concatenate([ix[2 * k:2 * k + 1], ix[2 * k + 1:2 * k + 2]], axis=1)
                    return (lax.broadcasted_iota(I32, (size, ROWS), 0) == row).astype(F32)

                group = one_hot(0, NGRP).astype(BF16)
                one, two = one_hot(1, A8), one_hot(2, A8)
                plus = (one + two).astype(BF16)
                minus = (one - two).astype(BF16)
                hot[j, 0:NGRP] = group
                hot[j, NGRP:NGRP + A8] = plus
                hot[j, NGRP + A8:HOT] = minus
                total[...] += nt(hot[j], jnp.concatenate([group, d], axis=0))
            else:
                sums[...] += nt(hot[j], d)

    def solve(n):
        if n == 0:
            sums[...] = total[:, NGRP:NGRP + 2 * OWN]
            count[...] = jnp.broadcast_to(
                jnp.sum(total[0:NGRP, 0:NGRP], axis=1, keepdims=True), (NGRP, 2 * OWN)
            )
        mean = sums[0:NGRP] / count[...]
        for s in (0, 1):
            rows = slice(NGRP + s * A8, NGRP + (s + 1) * A8)
            cols = slice(s * OWN, (s + 1) * OWN)
            rhs = sums[rows, cols] - jnp.dot(
                total[rows, 0:NGRP], mean[:, cols], precision=HIGH, preferred_element_type=F32
            )
            g = nt(rhs.T, inv[s], HIGH)
            shared[n, mx, mz, :, s * APAD:(s + 1) * APAD] = encode(g).astype(I16)
        if n + 1 < PARTS:
            clear(sums)

    started = []

    def begin(copy):
        copy.start()
        started.append(copy)

    def spread_start(n):
        for step in (1, -1, 2, -2):
            begin(b1(n, 0, step))
        for way in (0, 1):
            begin(b2(n, way, 0, mx))

    def spread_near(n):
        for sign in (-1, 1):
            b1_wait(n, 2 * sign)
            begin(b1(n, 2 * sign, -sign))
            begin(b1(n, 2 * sign, -2 * sign, half=0 if sign < 0 else 1))
            b1_wait(n, sign)
        for dz in (-1, 1, -2, 2):
            for way in (0, 1):
                begin(b2(n, way, dz, mx))

    def spread_far(n):
        for dz in (-3, 3):
            b1_wait(n, dz)
            for way in (0, 1):
                begin(b2(n, way, dz, mx))
        for half in (0, 1):
            b1_wait(n, 4, half=half)
        for way in (0, 1):
            begin(b2(n, way, 4, mx))

    order = (0, -1, 1, -2, 2, -3, 3, 4)

    def spread_across(n):
        for i, dz in enumerate(order):
            for way in (0, 1):
                source = x_of(2 * way - 1)
                b2(n, way, dz, source).wait_recv()
                if i % 2 == way:
                    begin(b3(n, way, dz, source))

    def spread_end(n):
        for i, dz in enumerate(order):
            b3(n, i % 2, dz, x_of(2)).wait_recv()

    def calibrate(n):
        @pl.loop(0, NX)
        def _(x):
            rows = pl.ds(pl.multiple_of(x * NZ * OWN, NZ * OWN), NZ * OWN)
            q = shared[n, x].reshape(NZ * OWN, 2 * APAD).astype(I32)
            for s in (0, 1):
                cols = slice(s * APAD, (s + 1) * APAD)
                part = q[:, cols]
                k = part[:, ANTENNA_COUNT:ANTENNA_COUNT + 1] - 15
                g = part.astype(F32) * jnp.exp2(k.astype(F32))
                high = g.astype(BF16)
                g_full[rows, cols] = g
                g_high[rows, cols] = high
                g_low[rows, cols] = (g - high.astype(F32)).astype(BF16)

        for s in (0, 1):
            cols = slice(s * APAD, (s + 1) * APAD)
            combo[s] = nt(select[s], g_high[:, cols]) + nt(select[s], g_low[:, cols])

        @pl.loop(0, NTA)
        def _(d):
            rows = pl.ds(pl.multiple_of(d * BASE, BASE), BASE)
            cols = slice(n * CW, (n + 1) * CW)
            u = amp[rows, cols].astype(F32) - combo[0, rows, :]
            v = ph[rows, cols].astype(F32) - combo[1, rows, :]
            magnitude = jnp.exp(u)
            sine, cosine = sin_cos(v)
            out_cal[n, d, 0] = (magnitude * cosine).astype(BF16)
            out_cal[n, d, 1] = (magnitude * sine).astype(BF16)

        @pl.loop(1, NTA)
        def _(j):
            cal_copy(n, j).start()

        in_cal[n, 0] = out_cal[n, mt]
        for s in (0, 1):
            @pl.loop(0, CW // TILE)
            def _(k):
                block = g_full[pl.ds(pl.multiple_of(k * TILE, TILE), TILE), s * APAD:(s + 1) * APAD]
                start = s * ANTENNA_COUNT * NTILE + n * (CW // TILE) + k
                gains[pl.ds(start, ANTENNA_COUNT, stride=NTILE), :] = block.T[0:ANTENNA_COUNT]

    def mask(n):
        @pl.loop(0, NTA)
        def _(j):
            @pl.when(j > 0)
            def _():
                cal_copy(n, j).wait_recv()

            row = pl.multiple_of(lax.rem(mt - j + NTA, NTA) * LINE, LINE)
            w = keep[:, n * CW:(n + 1) * CW].astype(BF16)
            for c in (0, 1):
                masked[pl.ds(row + c * BASE, BASE), EDGE + n * CW:EDGE + (n + 1) * CW] = (
                    in_cal[n, j, c] * w
                )

    def fill(low, high):
        @pl.loop(low, high)
        def _(p):
            lane = pl.multiple_of(p * PAIR, PAIR)
            mixed[...] = nt(masked[:, pl.ds(lane, WINDOW)], wide[...])

            @pl.loop(0, NT)
            def _(to):
                total = times[to, 0]
                value = times[to, 0] * mixed[0:LINE]
                for t in range(1, NT):
                    total = total + times[to, t]
                    value = value + times[to, t] * mixed[t * LINE:(t + 1) * LINE]
                ratio = rden[:, pl.ds(lane, PAIR)] * (1.0 / jnp.full((1, PAIR), total, F32))
                w = keep[:, pl.ds(lane, PAIR)]
                for c in (0, 1):
                    row = pl.multiple_of(to * LINE + c * BASE, BASE)
                    own = masked[pl.ds(row, BASE), pl.ds(pl.multiple_of(lane + EDGE, TILE), PAIR)]
                    result = jnp.where(
                        w > 0.5, own.astype(F32), value[c * BASE:(c + 1) * BASE] * ratio
                    )
                    for i in (0, 1):
                        start = c * BASE * NTILE * NT + (2 * p + i) * NT + to
                        filled[pl.ds(start, BASE, stride=NTILE * NT), :] = (
                            result[:, i * TILE:(i + 1) * TILE]
                        )

    add_sums(0, 0, NBL)
    solve(0)
    spread_start(0)
    add_sums(1, 0, 8)
    spread_near(0)
    add_sums(1, 8, 16)
    spread_far(0)
    add_sums(1, 16, 24)
    spread_across(0)
    add_sums(1, 24, NBL)
    solve(1)
    spread_start(1)
    spread_end(0)
    add_sums(2, 0, 8)
    spread_near(1)
    calibrate(0)
    add_sums(2, 8, 16)
    spread_far(1)
    add_sums(2, 16, 24)
    spread_across(1)
    add_sums(2, 24, NBL)
    solve(2)
    spread_start(2)
    spread_end(1)
    mask(0)
    spread_near(2)
    calibrate(1)
    spread_far(2)
    spread_across(2)
    mask(1)
    fill(0, 2)
    spread_end(2)
    calibrate(2)
    mask(2)
    fill(2, NTILE // 2)

    for copy in started:
        copy.wait_send()

    @pl.loop(1, NBL)
    def _(j):
        index_copy(j).wait_send()
        for n in range(PARTS):
            data_copy(n, j).wait_send()

    @pl.loop(1, NTA)
    def _(j):
        for n in range(PARTS):
            cal_copy(n, j).wait_send()


def calibrate_and_fill(amp, ph, group_row, couples, flags, times, channel, inverse):
    dma = pltpu.SemaphoreType.DMA
    vmem = pl.BlockSpec(memory_space=pltpu.VMEM)
    smem = pl.BlockSpec(memory_space=pltpu.SMEM)
    return pl.pallas_call(
        whole_kernel,
        name="calibrate_and_fill",
        out_shape=(
            jax.ShapeDtypeStruct((2 * ANTENNA_COUNT * NTILE, TILE), F32),
            jax.ShapeDtypeStruct((2 * BASE * NTILE * NT, TILE), F32),
        ),
        in_specs=[vmem] * 5 + [smem, vmem, vmem],
        out_specs=(vmem, vmem),
        scratch_shapes=[
            pltpu.VMEM((PARTS, NBL, 2 * OWN, ROWS), BF16),
            pltpu.VMEM((PARTS, NBL, 2 * OWN, ROWS), BF16),
            pltpu.VMEM((8, 128), I16),
            pltpu.VMEM((NBL, 8, 128), I16),
            pltpu.VMEM((NBL, HOT, ROWS), BF16),
            pltpu.VMEM((2, APAD, A8), F32),
            pltpu.VMEM((HOT, NGRP + 2 * OWN), F32),
            pltpu.VMEM((HOT, 2 * OWN), F32),
            pltpu.VMEM((NGRP, 2 * OWN), F32),
            pltpu.VMEM((PARTS, NX, NZ, OWN, 2 * APAD), I16),
            pltpu.VMEM((CW, 2 * APAD), F32),
            pltpu.VMEM((CW, 2 * APAD), BF16),
            pltpu.VMEM((CW, 2 * APAD), BF16),
            pltpu.VMEM((2, ROWS, APAD), BF16),
            pltpu.VMEM((2, ROWS, CW), F32),
            pltpu.VMEM((PAIR, WINDOW), BF16),
            pltpu.VMEM((BASE, CH), F32),
            pltpu.VMEM((BASE, CH + 2 * EDGE), BF16),
            pltpu.VMEM((NT * LINE, CH + 2 * EDGE), BF16),
            pltpu.VMEM((BASE, CH), F32),
            pltpu.VMEM((NT * LINE, PAIR), F32),
            pltpu.VMEM((PARTS, NTA, 2, BASE, CW), BF16),
            pltpu.VMEM((PARTS, NTA, 2, BASE, CW), BF16),
            dma((NBL,)), dma((NBL,)), dma((PARTS, NBL)), dma((PARTS, NBL)),
            dma((PARTS, NZ)), dma((PARTS, NZ)), dma((PARTS, 2, NZ)), dma((PARTS, 2, NZ)),
            dma((PARTS, NZ)), dma((PARTS, NZ)), dma((PARTS, NTA)), dma((PARTS, NTA)),
        ],
        compiler_params=pltpu.CompilerParams(
            collective_id=0, has_side_effects=True, vmem_limit_bytes=56 * 2**20
        ),
    )(amp, ph, group_row, couples, flags, times, channel, inverse)


def copy_kernel(a, out):
    out[...] = a[...]


def copy_out(a):
    spec = pl.BlockSpec((a.shape[0] // 10, TILE), lambda i: (i, 0))
    return pl.pallas_call(
        copy_kernel,
        name="copy_out",
        grid=(10,),
        out_shape=jax.ShapeDtypeStruct(a.shape, a.dtype),
        in_specs=[spec],
        out_specs=spec,
    )(a)


def on_device(
    log_amplitude,
    phase,
    redundant_group_index,
    antenna_couples,
    tile_flag_mask,
    inverse,
    integration_kernel,
    channel_kernel,
):
    gains, filled = calibrate_and_fill(
        log_amplitude[:, 0], phase[:, 0], redundant_group_index[None, :], antenna_couples.T,
        tile_flag_mask.T, integration_kernel, channel_kernel, inverse.transpose(1, 0, 2),
    )
    gains = copy_out(gains)
    return (
        gains.reshape(2, ANTENNA_COUNT, 1, CH),
        filled.reshape(2, BASE, NTILE, NT, TILE).transpose(0, 1, 3, 2, 4).reshape(2, BASE, NT, CH),
    )


def solution(mesh):
    in_specs = (
        P("bl", "ta", None),
        P("bl", "ta", None),
        P("bl"),
        P("bl", None),
        P(("bl", "ta"), None),
        P(),
        P(),
        P(),
    )
    out_specs = (P(None, None, "ta", None), P(None, ("bl", "ta"), None, None))
    return jax.shard_map(
        on_device, mesh=mesh, in_specs=in_specs, out_specs=out_specs, check_vma=False
    )
```

```python
import jax
import jax.numpy as jnp
from jax import lax
from jax.experimental import pallas as pl
from jax.experimental.pallas import tpu as pltpu
from jax.sharding import PartitionSpec as P

ANTENNA_COUNT = 350
NGRP = 224
TILE = 128
REACH = 3
HIGH = lax.Precision.HIGHEST
F32 = jnp.float32
BF16 = jnp.bfloat16
I16 = jnp.int16
I32 = jnp.int32
MESH = pl.DeviceIdType.MESH

NX, NZ = 4, 8
NBL = NX * NZ
NTA = 8
NT = 8
ROWS = 256
BASE = ROWS // NTA
CH = 1536
PARTS = 3
CW = CH // PARTS
OWN = CW // NBL
APAD = 384
A8 = 352
HOT = NGRP + 2 * A8
NTILE = CH // TILE
PAIR = 2 * TILE
WINDOW = 8 * TILE
EDGE = REACH * TILE
LINE = 2 * BASE
MINE = PARTS * OWN


def nt(a, b, precision=None):
    return lax.dot_general(
        a, b, (((1,), (1,)), ((), ())), preferred_element_type=F32, precision=precision
    )


def encode(g):
    peak = jnp.max(jnp.abs(g), axis=1, keepdims=True)
    k = jnp.floor(jnp.log2(jnp.maximum(peak, F32(2.0**-100)))).astype(I32) + 2
    coded = jnp.round(g * jnp.exp2((15 - k).astype(F32))).astype(I32)
    lane = lax.broadcasted_iota(I32, g.shape, 1)
    return jnp.where(lane == ANTENNA_COUNT, k, coded)


def sin_cos(v):
    n = jnp.round(v * F32(0.6366197723675814))
    r = v - n * F32(1.5703125)
    r = r - n * F32(4.837512969970703125e-4)
    r = r - n * F32(7.54978995489188216e-8)
    quadrant = n.astype(I32)
    z = r * r
    s = ((F32(-1.9515295891e-4) * z + F32(8.3321608736e-3)) * z - F32(1.6666654611e-1)) * z * r + r
    c = (
        (F32(2.443315711809948e-5) * z - F32(1.388731625493765e-3)) * z + F32(4.166664568298827e-2)
    ) * z * z - F32(0.5) * z + F32(1.0)
    swap = (quadrant & 1) != 0
    sine = jnp.where(swap, c, s)
    cosine = jnp.where(swap, s, c)
    sine = jnp.where((quadrant & 2) != 0, -sine, sine)
    cosine = jnp.where(((quadrant + 1) & 2) != 0, -cosine, cosine)
    return sine, cosine


def whole_kernel(
    amp, ph, group_row, couples, flags, times, channel, inverse, gains, filled,
    send, got, index, got_index, inv, total, shared,
    g_full, g_high, g_low, select, combo, wide, keep, keep_wide, masked, rden, mixed,
    out_cal, in_cal,
    index_send, index_recv, data_send, data_recv, b1_send, b1_recv, b2_send, b2_recv,
    b3_send, b3_recv, cal_send, cal_recv,
):
    me = lax.axis_index("bl")
    mx, mz = me // NZ, lax.rem(me, NZ)
    mt = lax.axis_index("ta")

    def x_of(dx):
        return lax.rem(mx + dx + NX, NX)

    def z_of(dz):
        return lax.rem(mz + dz + NZ, NZ)

    def device(dx, dz):
        return x_of(dx) * NZ + z_of(dz)

    def peer_of(j):
        return device(j // NZ, lax.rem(3 * j, NZ))

    def time_peer(j):
        return lax.rem(mt + j, NTA)

    def remote(src, dst, send_sem, recv_sem, axis, peer):
        return pltpu.make_async_remote_copy(
            src_ref=src, dst_ref=dst, send_sem=send_sem, recv_sem=recv_sem,
            device_id={axis: peer}, device_id_type=MESH,
        )

    def index_copy(j):
        return remote(
            index, got_index.at[j], index_send.at[j], index_recv.at[j], "bl", peer_of(j)
        )

    def data_copy(j):
        peer = peer_of(j)
        return remote(send.at[peer], got.at[j], data_send.at[j], data_recv.at[j], "bl", peer)

    def cal_copy(n, j):
        peer = time_peer(j)
        return remote(
            out_cal.at[n, peer], in_cal.at[n, j], cal_send.at[n, j], cal_recv.at[n, j], "ta", peer
        )

    def b1(n, dz, step, half=None):
        slot = shared.at[n, mx, z_of(dz)]
        number = (step - dz) % NZ
        if half is not None:
            slot = slot.at[:, pl.ds(half * APAD, APAD)]
            number = 4 * half
        return remote(slot, slot, b1_send.at[n, number], b1_recv.at[n, number], "bl", device(0, step))

    def b1_wait(n, dz, half=None):
        slot = shared.at[n, mx, z_of(dz)]
        number = (-dz) % NZ
        if half is not None:
            slot = slot.at[:, pl.ds(half * APAD, APAD)]
            number = 4 * half
        remote(slot, slot, b1_send.at[n, number], b1_recv.at[n, number], "bl", device(0, 1)).wait_recv()

    def b2(n, way, dz, src_x):
        slot = shared.at[n, src_x, z_of(dz)]
        number = dz % NZ
        return remote(
            slot, slot, b2_send.at[n, way, number], b2_recv.at[n, way, number],
            "bl", device(1 - 2 * way, 0),
        )

    def b3(n, way, dz, src_x):
        slot = shared.at[n, src_x, z_of(dz)]
        number = dz % NZ
        return remote(
            slot, slot, b3_send.at[n, number], b3_recv.at[n, number], "bl", device(1 - 2 * way, 0)
        )

    barrier = pltpu.get_barrier_semaphore()

    @pl.loop(1, NBL)
    def _(j):
        pl.semaphore_signal(barrier, inc=1, device_id={"bl": peer_of(j)}, device_id_type=MESH)

    @pl.loop(1, NTA)
    def _(j):
        pl.semaphore_signal(barrier, inc=1, device_id={"ta": time_peer(j)}, device_id_type=MESH)

    def turn(n):
        cols = slice(n * CW, (n + 1) * CW)
        for s, ref in enumerate((amp, ph)):
            first = s * MINE + n * OWN
            send[:, first:first + OWN, :] = ref[:, cols].T.reshape(NBL, OWN, ROWS)

    index[...] = jnp.concatenate(
        [
            ref[k:k + 1, h * TILE:(h + 1) * TILE]
            for ref, k in ((group_row, 0), (couples, 0), (couples, 1)) for h in (0, 1)
        ] + [jnp.zeros((2, TILE), I32)], axis=0
    ).astype(I16)
    for n in range(PARTS):
        turn(n)
    pl.semaphore_wait(barrier, NBL - 1 + NTA - 1)

    @pl.loop(1, NBL)
    def _(j):
        index_copy(j).start()

    @pl.loop(1, NBL)
    def _(j):
        data_copy(j).start()

    got[0] = send[me]
    got_index[0] = index[...]
    inv[...] = jnp.zeros_like(inv)
    for s in (0, 1):
        inv[s, 0:ANTENNA_COUNT, 0:ANTENNA_COUNT] = inverse[:, s, :]
    label = lax.broadcasted_iota(I32, (APAD, ROWS), 0)
    first = (couples[0:1, :] == label).astype(F32)
    second = (couples[1:2, :] == label).astype(F32)
    select[0] = (first + second).T.astype(BF16)
    select[1] = (first - second).T.astype(BF16)
    wide[...] = jnp.zeros_like(wide)
    for c in (0, 1):
        for o in range(2 * REACH + 1):
            wide[c * TILE:(c + 1) * TILE, (c + o) * TILE:(c + o + 1) * TILE] = channel[o]
    masked[...] = jnp.zeros_like(masked)
    keep_wide[...] = jnp.zeros_like(keep_wide)
    tile = lax.broadcasted_iota(I32, (NTILE, CH), 1) // TILE
    spread = (tile == lax.broadcasted_iota(I32, (NTILE, CH), 0)).astype(F32).astype(BF16)
    open_tiles = (1 - flags[...]).astype(F32).astype(BF16)
    keep[...] = lax.dot_general(
        open_tiles, spread, (((0,), (0,)), ((), ())), preferred_element_type=F32
    )
    keep_wide[:, EDGE:EDGE + CH] = keep[...].astype(BF16)
    for p in range(NTILE // 2):
        rden[:, PAIR * p:PAIR * (p + 1)] = 1.0 / nt(
            keep_wide[:, PAIR * p:PAIR * p + WINDOW], wide[...]
        )

    def clear(*refs):
        for ref in refs:
            ref[...] = jnp.zeros_like(ref)

    clear(total)

    def add_sums():
        @pl.loop(0, NBL)
        def _(j):
            @pl.when(j > 0)
            def _():
                index_copy(j).wait_recv()
                data_copy(j).wait_recv()

            ix = got_index[j].astype(I32)

            def one_hot(k, size):
                row = jnp.concatenate([ix[2 * k:2 * k + 1], ix[2 * k + 1:2 * k + 2]], axis=1)
                return (lax.broadcasted_iota(I32, (size, ROWS), 0) == row).astype(F32)

            group = one_hot(0, NGRP).astype(BF16)
            one, two = one_hot(1, A8), one_hot(2, A8)
            hot = jnp.concatenate(
                [group, (one + two).astype(BF16), (one - two).astype(BF16)], axis=0
            )
            total[...] += nt(hot, jnp.concatenate([group, got[j]], axis=0))

    def solve():
        count = jnp.sum(total[0:NGRP, 0:NGRP], axis=1, keepdims=True)
        mean = total[0:NGRP, NGRP:NGRP + 2 * MINE] / count
        for s in (0, 1):
            rows = slice(NGRP + s * A8, NGRP + (s + 1) * A8)
            cols = slice(s * MINE, (s + 1) * MINE)
            rhs = total[rows, NGRP + s * MINE:NGRP + (s + 1) * MINE] - jnp.dot(
                total[rows, 0:NGRP], mean[:, cols], precision=HIGH, preferred_element_type=F32
            )
            coded = encode(nt(rhs.T, inv[s], HIGH)).astype(I16)
            for n in range(PARTS):
                shared[n, mx, mz, :, s * APAD:(s + 1) * APAD] = coded[n * OWN:(n + 1) * OWN]

    started = []

    def begin(copy):
        copy.start()
        started.append(copy)

    def spread_start(n):
        for step in (1, -1, 2, -2):
            begin(b1(n, 0, step))
        for way in (0, 1):
            begin(b2(n, way, 0, mx))

    def spread_near(n):
        for sign in (-1, 1):
            b1_wait(n, sign)
            for way in (0, 1):
                begin(b2(n, way, sign, mx))
        for sign in (-1, 1):
            b1_wait(n, 2 * sign)
            begin(b1(n, 2 * sign, -sign))
            begin(b1(n, 2 * sign, -2 * sign, half=0 if sign < 0 else 1))
            for way in (0, 1):
                begin(b2(n, way, 2 * sign, mx))

    def spread_far(n):
        for dz in (-3, 3):
            b1_wait(n, dz)
            for way in (0, 1):
                begin(b2(n, way, dz, mx))
        for half in (0, 1):
            b1_wait(n, 4, half=half)
        for way in (0, 1):
            begin(b2(n, way, 4, mx))

    order = (0, -1, 1, -2, 2, -3, 3, 4)

    def spread_across(n):
        for i, dz in enumerate(order):
            for way in (0, 1):
                source = x_of(2 * way - 1)
                b2(n, way, dz, source).wait_recv()
                if i % 2 == way:
                    begin(b3(n, way, dz, source))

    def spread_end(n):
        for i, dz in enumerate(order):
            b3(n, i % 2, dz, x_of(2)).wait_recv()

    def calibrate(n):
        @pl.loop(0, NX)
        def _(x):
            rows = pl.ds(pl.multiple_of(x * NZ * OWN, NZ * OWN), NZ * OWN)
            q = shared[n, x].reshape(NZ * OWN, 2 * APAD).astype(I32)
            for s in (0, 1):
                cols = slice(s * APAD, (s + 1) * APAD)
                part = q[:, cols]
                k = part[:, ANTENNA_COUNT:ANTENNA_COUNT + 1] - 15
                g = part.astype(F32) * jnp.exp2(k.astype(F32))
                high = g.astype(BF16)
                g_full[rows, cols] = g
                g_high[rows, cols] = high
                g_low[rows, cols] = (g - high.astype(F32)).astype(BF16)

        for s in (0, 1):
            cols = slice(s * APAD, (s + 1) * APAD)
            combo[s] = nt(select[s], g_high[:, cols]) + nt(select[s], g_low[:, cols])

        @pl.loop(1, NTA + 1)
        def _(j):
            d = time_peer(j)
            rows = pl.ds(pl.multiple_of(d * BASE, BASE), BASE)
            cols = slice(n * CW, (n + 1) * CW)
            u = amp[rows, cols].astype(F32) - combo[0, rows, :]
            v = ph[rows, cols].astype(F32) - combo[1, rows, :]
            magnitude = jnp.exp(u)
            sine, cosine = sin_cos(v)
            out_cal[n, d, 0] = (magnitude * cosine).astype(BF16)
            out_cal[n, d, 1] = (magnitude * sine).astype(BF16)

            @pl.when(j < NTA)
            def _():
                cal_copy(n, j).start()

        in_cal[n, 0] = out_cal[n, mt]
        for s in (0, 1):
            @pl.loop(0, CW // TILE)
            def _(k):
                block = g_full[pl.ds(pl.multiple_of(k * TILE, TILE), TILE), s * APAD:(s + 1) * APAD]
                start = s * ANTENNA_COUNT * NTILE + n * (CW // TILE) + k
                gains[pl.ds(start, ANTENNA_COUNT, stride=NTILE), :] = block.T[0:ANTENNA_COUNT]

    def mask(n):
        @pl.loop(0, NTA)
        def _(j):
            @pl.when(j > 0)
            def _():
                cal_copy(n, j).wait_recv()

            row = pl.multiple_of(lax.rem(mt - j + NTA, NTA) * LINE, LINE)
            w = keep[:, n * CW:(n + 1) * CW].astype(BF16)
            for c in (0, 1):
                masked[pl.ds(row + c * BASE, BASE), EDGE + n * CW:EDGE + (n + 1) * CW] = (
                    in_cal[n, j, c] * w
                )

    def fill(low, high):
        @pl.loop(low, high)
        def _(p):
            lane = pl.multiple_of(p * PAIR, PAIR)
            mixed[...] = nt(masked[:, pl.ds(lane, WINDOW)], wide[...])

            @pl.loop(0, NT)
            def _(to):
                total = times[to, 0]
                value = times[to, 0] * mixed[0:LINE]
                for t in range(1, NT):
                    total = total + times[to, t]
                    value = value + times[to, t] * mixed[t * LINE:(t + 1) * LINE]
                ratio = rden[:, pl.ds(lane, PAIR)] * (1.0 / jnp.full((1, PAIR), total, F32))
                w = keep[:, pl.ds(lane, PAIR)]
                for c in (0, 1):
                    row = pl.multiple_of(to * LINE + c * BASE, BASE)
                    own = masked[pl.ds(row, BASE), pl.ds(pl.multiple_of(lane + EDGE, TILE), PAIR)]
                    result = jnp.where(
                        w > 0.5, own.astype(F32), value[c * BASE:(c + 1) * BASE] * ratio
                    )
                    for i in (0, 1):
                        start = c * BASE * NTILE * NT + (2 * p + i) * NT + to
                        filled[pl.ds(start, BASE, stride=NTILE * NT), :] = (
                            result[:, i * TILE:(i + 1) * TILE]
                        )

    add_sums()
    solve()
    for n in range(PARTS):
        spread_start(n)
    spread_near(0)
    spread_near(1)
    spread_far(0)
    spread_near(2)
    spread_far(1)
    spread_across(0)
    spread_far(2)
    spread_across(1)
    spread_end(0)
    calibrate(0)
    spread_across(2)
    spread_end(1)
    calibrate(1)
    mask(0)
    mask(1)
    fill(0, 2)
    spread_end(2)
    calibrate(2)
    mask(2)
    fill(2, NTILE // 2)

    for copy in started:
        copy.wait_send()

    @pl.loop(1, NBL)
    def _(j):
        index_copy(j).wait_send()
        data_copy(j).wait_send()

    @pl.loop(1, NTA)
    def _(j):
        for n in range(PARTS):
            cal_copy(n, j).wait_send()


def calibrate_and_fill(amp, ph, group_row, couples, flags, times, channel, inverse):
    dma = pltpu.SemaphoreType.DMA
    vmem = pl.BlockSpec(memory_space=pltpu.VMEM)
    smem = pl.BlockSpec(memory_space=pltpu.SMEM)
    return pl.pallas_call(
        whole_kernel,
        name="calibrate_and_fill",
        out_shape=(
            jax.ShapeDtypeStruct((2 * ANTENNA_COUNT * NTILE, TILE), F32),
            jax.ShapeDtypeStruct((2 * BASE * NTILE * NT, TILE), F32),
        ),
        in_specs=[vmem] * 5 + [smem, vmem, vmem],
        out_specs=(vmem, vmem),
        scratch_shapes=[
            pltpu.VMEM((NBL, 2 * MINE, ROWS), BF16),
            pltpu.VMEM((NBL, 2 * MINE, ROWS), BF16),
            pltpu.VMEM((8, 128), I16),
            pltpu.VMEM((NBL, 8, 128), I16),
            pltpu.VMEM((2, APAD, A8), F32),
            pltpu.VMEM((HOT, NGRP + 2 * MINE), F32),
            pltpu.VMEM((PARTS, NX, NZ, OWN, 2 * APAD), I16),
            pltpu.VMEM((CW, 2 * APAD), F32),
            pltpu.VMEM((CW, 2 * APAD), BF16),
            pltpu.VMEM((CW, 2 * APAD), BF16),
            pltpu.VMEM((2, ROWS, APAD), BF16),
            pltpu.VMEM((2, ROWS, CW), F32),
            pltpu.VMEM((PAIR, WINDOW), BF16),
            pltpu.VMEM((BASE, CH), F32),
            pltpu.VMEM((BASE, CH + 2 * EDGE), BF16),
            pltpu.VMEM((NT * LINE, CH + 2 * EDGE), BF16),
            pltpu.VMEM((BASE, CH), F32),
            pltpu.VMEM((NT * LINE, PAIR), F32),
            pltpu.VMEM((PARTS, NTA, 2, BASE, CW), BF16),
            pltpu.VMEM((PARTS, NTA, 2, BASE, CW), BF16),
            dma((NBL,)), dma((NBL,)), dma((NBL,)), dma((NBL,)),
            dma((PARTS, NZ)), dma((PARTS, NZ)), dma((PARTS, 2, NZ)), dma((PARTS, 2, NZ)),
            dma((PARTS, NZ)), dma((PARTS, NZ)), dma((PARTS, NTA)), dma((PARTS, NTA)),
        ],
        compiler_params=pltpu.CompilerParams(
            collective_id=0, has_side_effects=True, vmem_limit_bytes=40 * 2**20
        ),
    )(amp, ph, group_row, couples, flags, times, channel, inverse)


def copy_kernel(a, b, out_a, out_b, sem):
    copies = []
    for k, (src, dst) in enumerate(((a, out_a), (b, out_b))):
        size = src.shape[0] // 2
        for i in range(2):
            rows = pl.ds(i * size, size)
            copies.append(pltpu.make_async_copy(src.at[rows], dst.at[rows], sem.at[k, i]))
    for copy in copies:
        copy.start()
    for copy in copies:
        copy.wait()


def copy_out(a, b):
    return pl.pallas_call(
        copy_kernel,
        name="copy_out",
        out_shape=(
            jax.ShapeDtypeStruct(a.shape, a.dtype), jax.ShapeDtypeStruct(b.shape, b.dtype)
        ),
        in_specs=[pl.BlockSpec(memory_space=pltpu.VMEM)] * 2,
        out_specs=(pl.BlockSpec(memory_space=pl.ANY),) * 2,
        scratch_shapes=[pltpu.SemaphoreType.DMA((2, 2))],
        compiler_params=pltpu.CompilerParams(vmem_limit_bytes=10 * 2**20),
    )(a, b)


def on_device(
    log_amplitude,
    phase,
    redundant_group_index,
    antenna_couples,
    tile_flag_mask,
    inverse,
    integration_kernel,
    channel_kernel,
):
    gains, filled = copy_out(*calibrate_and_fill(
        log_amplitude[:, 0], phase[:, 0], redundant_group_index[None, :], antenna_couples.T,
        tile_flag_mask.T, integration_kernel, channel_kernel, inverse.transpose(1, 0, 2),
    ))
    return (
        gains.reshape(2, ANTENNA_COUNT, 1, CH),
        filled.reshape(2, BASE, NTILE, NT, TILE).transpose(0, 1, 3, 2, 4).reshape(2, BASE, NT, CH),
    )


def solution(mesh):
    in_specs = (
        P("bl", "ta", None),
        P("bl", "ta", None),
        P("bl"),
        P("bl", None),
        P(("bl", "ta"), None),
        P(),
        P(),
        P(),
    )
    out_specs = (P(None, None, "ta", None), P(None, ("bl", "ta"), None, None))
    return jax.shard_map(
        on_device, mesh=mesh, in_specs=in_specs, out_specs=out_specs, check_vma=False
    )
```

```python
import jax
import jax.numpy as jnp
from jax import lax
from jax.experimental import pallas as pl
from jax.experimental.pallas import tpu as pltpu
from jax.sharding import PartitionSpec as P

ANTENNA_COUNT = 350
NGRP = 224
TILE = 128
REACH = 3
HIGH = lax.Precision.HIGHEST
F32 = jnp.float32
BF16 = jnp.bfloat16
I16 = jnp.int16
I32 = jnp.int32
MESH = pl.DeviceIdType.MESH

NX, NZ = 4, 8
NBL = NX * NZ
NTA = 8
NT = 8
ROWS = 256
BASE = ROWS // NTA
CH = 1536
PARTS = 3
CW = CH // PARTS
OWN = CW // NBL
APAD = 384
A8 = 352
HOT = NGRP + 2 * A8
NTILE = CH // TILE
PAIR = 2 * TILE
WINDOW = 8 * TILE
EDGE = REACH * TILE
LINE = 2 * BASE
MINE = PARTS * OWN


def nt(a, b, precision=None):
    return lax.dot_general(
        a, b, (((1,), (1,)), ((), ())), preferred_element_type=F32, precision=precision
    )


def encode(g):
    peak = jnp.max(jnp.abs(g), axis=1, keepdims=True)
    k = jnp.floor(jnp.log2(jnp.maximum(peak, F32(2.0**-100)))).astype(I32) + 2
    coded = jnp.round(g * jnp.exp2((15 - k).astype(F32))).astype(I32)
    lane = lax.broadcasted_iota(I32, g.shape, 1)
    return jnp.where(lane == ANTENNA_COUNT, k, coded)


def sin_cos(v):
    n = jnp.round(v * F32(0.6366197723675814))
    r = v - n * F32(1.5703125)
    r = r - n * F32(4.837512969970703125e-4)
    r = r - n * F32(7.54978995489188216e-8)
    quadrant = n.astype(I32)
    z = r * r
    s = ((F32(-1.9515295891e-4) * z + F32(8.3321608736e-3)) * z - F32(1.6666654611e-1)) * z * r + r
    c = (
        (F32(2.443315711809948e-5) * z - F32(1.388731625493765e-3)) * z + F32(4.166664568298827e-2)
    ) * z * z - F32(0.5) * z + F32(1.0)
    swap = (quadrant & 1) != 0
    sine = jnp.where(swap, c, s)
    cosine = jnp.where(swap, s, c)
    sine = jnp.where((quadrant & 2) != 0, -sine, sine)
    cosine = jnp.where(((quadrant + 1) & 2) != 0, -cosine, cosine)
    return sine, cosine


def whole_kernel(
    amp_in, ph_in, group_in, couples_in, flags_in, times_in, channel_in, inverse_in, gains, filled,
    amp, ph, group_row, couples, flags, times, channel, inverse, in_sem, send, got, index, got_index, inv, total, shared,
    g_full, g_high, g_low, select, combo, wide, keep, keep_wide, masked, rden, mixed,
    out_cal, in_cal,
    index_send, index_recv, data_send, data_recv, b1_send, b1_recv, b2_send, b2_recv,
    b3_send, b3_recv, cal_send, cal_recv,
):
    me = lax.axis_index("bl")
    mx, mz = me // NZ, lax.rem(me, NZ)
    mt = lax.axis_index("ta")

    def x_of(dx):
        return lax.rem(mx + dx + NX, NX)

    def z_of(dz):
        return lax.rem(mz + dz + NZ, NZ)

    def device(dx, dz):
        return x_of(dx) * NZ + z_of(dz)

    def peer_of(j):
        return device(j // NZ, lax.rem(3 * j, NZ))

    def time_peer(j):
        return lax.rem(mt + j, NTA)

    def remote(src, dst, send_sem, recv_sem, axis, peer):
        return pltpu.make_async_remote_copy(
            src_ref=src, dst_ref=dst, send_sem=send_sem, recv_sem=recv_sem,
            device_id={axis: peer}, device_id_type=MESH,
        )

    def index_copy(j):
        return remote(
            index, got_index.at[j], index_send.at[j], index_recv.at[j], "bl", peer_of(j)
        )

    def data_copy(j):
        peer = peer_of(j)
        return remote(send.at[peer], got.at[j], data_send.at[j], data_recv.at[j], "bl", peer)

    def cal_copy(n, j):
        peer = time_peer(j)
        return remote(
            out_cal.at[n, peer], in_cal.at[n, j], cal_send.at[n, j], cal_recv.at[n, j], "ta", peer
        )

    def b1(n, dz, step, half=None):
        slot = shared.at[n, mx, z_of(dz)]
        number = (step - dz) % NZ
        if half is not None:
            slot = slot.at[:, pl.ds(half * APAD, APAD)]
            number = 4 * half
        return remote(slot, slot, b1_send.at[n, number], b1_recv.at[n, number], "bl", device(0, step))

    def b1_wait(n, dz, half=None):
        slot = shared.at[n, mx, z_of(dz)]
        number = (-dz) % NZ
        if half is not None:
            slot = slot.at[:, pl.ds(half * APAD, APAD)]
            number = 4 * half
        remote(slot, slot, b1_send.at[n, number], b1_recv.at[n, number], "bl", device(0, 1)).wait_recv()

    def b2(n, way, dz, src_x):
        slot = shared.at[n, src_x, z_of(dz)]
        number = dz % NZ
        return remote(
            slot, slot, b2_send.at[n, way, number], b2_recv.at[n, way, number],
            "bl", device(1 - 2 * way, 0),
        )

    def b3(n, way, dz, src_x):
        slot = shared.at[n, src_x, z_of(dz)]
        number = dz % NZ
        return remote(
            slot, slot, b3_send.at[n, number], b3_recv.at[n, number], "bl", device(1 - 2 * way, 0)
        )

    incoming = [
        pltpu.make_async_copy(src, dst, in_sem.at[k])
        for k, (src, dst) in enumerate((
            (amp_in, amp), (ph_in, ph), (group_in, group_row), (couples_in, couples),
            (flags_in, flags), (times_in, times), (channel_in, channel), (inverse_in, inverse),
        ))
    ]
    for copy in incoming:
        copy.start()
    barrier = pltpu.get_barrier_semaphore()

    @pl.loop(1, NBL)
    def _(j):
        pl.semaphore_signal(barrier, inc=1, device_id={"bl": peer_of(j)}, device_id_type=MESH)

    @pl.loop(1, NTA)
    def _(j):
        pl.semaphore_signal(barrier, inc=1, device_id={"ta": time_peer(j)}, device_id_type=MESH)

    def turn(n):
        cols = slice(n * CW, (n + 1) * CW)
        for s, ref in enumerate((amp, ph)):
            first = s * MINE + n * OWN
            send[:, first:first + OWN, :] = ref[:, cols].T.reshape(NBL, OWN, ROWS)

    for copy in incoming[:4]:
        copy.wait()
    index[...] = jnp.concatenate(
        [
            ref[k:k + 1, h * TILE:(h + 1) * TILE]
            for ref, k in ((group_row, 0), (couples, 0), (couples, 1)) for h in (0, 1)
        ] + [jnp.zeros((2, TILE), I32)], axis=0
    ).astype(I16)
    for n in range(PARTS):
        turn(n)
    pl.semaphore_wait(barrier, NBL - 1 + NTA - 1)

    @pl.loop(1, NBL)
    def _(j):
        index_copy(j).start()

    @pl.loop(1, NBL)
    def _(j):
        data_copy(j).start()

    for copy in incoming[4:]:
        copy.wait()
    got[0] = send[me]
    got_index[0] = index[...]
    inv[...] = jnp.zeros_like(inv)
    for s in (0, 1):
        inv[s, 0:ANTENNA_COUNT, 0:ANTENNA_COUNT] = inverse[:, s, :]
    label = lax.broadcasted_iota(I32, (APAD, ROWS), 0)
    first = (couples[0:1, :] == label).astype(F32)
    second = (couples[1:2, :] == label).astype(F32)
    select[0] = (first + second).T.astype(BF16)
    select[1] = (first - second).T.astype(BF16)
    wide[...] = jnp.zeros_like(wide)
    for c in (0, 1):
        for o in range(2 * REACH + 1):
            wide[c * TILE:(c + 1) * TILE, (c + o) * TILE:(c + o + 1) * TILE] = channel[o]
    masked[...] = jnp.zeros_like(masked)
    keep_wide[...] = jnp.zeros_like(keep_wide)
    tile = lax.broadcasted_iota(I32, (NTILE, CH), 1) // TILE
    spread = (tile == lax.broadcasted_iota(I32, (NTILE, CH), 0)).astype(F32).astype(BF16)
    open_tiles = (1 - flags[...]).astype(F32).astype(BF16)
    keep[...] = lax.dot_general(
        open_tiles, spread, (((0,), (0,)), ((), ())), preferred_element_type=F32
    )
    keep_wide[:, EDGE:EDGE + CH] = keep[...].astype(BF16)
    for p in range(NTILE // 2):
        rden[:, PAIR * p:PAIR * (p + 1)] = 1.0 / nt(
            keep_wide[:, PAIR * p:PAIR * p + WINDOW], wide[...]
        )

    def clear(*refs):
        for ref in refs:
            ref[...] = jnp.zeros_like(ref)

    clear(total)

    def add_sums():
        @pl.loop(0, NBL)
        def _(j):
            @pl.when(j > 0)
            def _():
                index_copy(j).wait_recv()
                data_copy(j).wait_recv()

            ix = got_index[j].astype(I32)

            def one_hot(k, size):
                row = jnp.concatenate([ix[2 * k:2 * k + 1], ix[2 * k + 1:2 * k + 2]], axis=1)
                return (lax.broadcasted_iota(I32, (size, ROWS), 0) == row).astype(F32)

            group = one_hot(0, NGRP).astype(BF16)
            one, two = one_hot(1, A8), one_hot(2, A8)
            hot = jnp.concatenate(
                [group, (one + two).astype(BF16), (one - two).astype(BF16)], axis=0
            )
            total[...] += nt(hot, jnp.concatenate([group, got[j]], axis=0))

    def solve():
        count = jnp.sum(total[0:NGRP, 0:NGRP], axis=1, keepdims=True)
        mean = total[0:NGRP, NGRP:NGRP + 2 * MINE] / count
        for s in (0, 1):
            rows = slice(NGRP + s * A8, NGRP + (s + 1) * A8)
            cols = slice(s * MINE, (s + 1) * MINE)
            rhs = total[rows, NGRP + s * MINE:NGRP + (s + 1) * MINE] - jnp.dot(
                total[rows, 0:NGRP], mean[:, cols], precision=HIGH, preferred_element_type=F32
            )
            coded = encode(nt(rhs.T, inv[s], HIGH)).astype(I16)
            for n in range(PARTS):
                shared[n, mx, mz, :, s * APAD:(s + 1) * APAD] = coded[n * OWN:(n + 1) * OWN]

    started = []

    def begin(copy):
        copy.start()
        started.append(copy)

    def spread_start(n):
        for step in (1, -1, 2, -2):
            begin(b1(n, 0, step))
        for way in (0, 1):
            begin(b2(n, way, 0, mx))

    def spread_near(n):
        for sign in (-1, 1):
            b1_wait(n, sign)
            for way in (0, 1):
                begin(b2(n, way, sign, mx))
        for sign in (-1, 1):
            b1_wait(n, 2 * sign)
            begin(b1(n, 2 * sign, -sign))
            begin(b1(n, 2 * sign, -2 * sign, half=0 if sign < 0 else 1))
            for way in (0, 1):
                begin(b2(n, way, 2 * sign, mx))

    def spread_far(n):
        for dz in (-3, 3):
            b1_wait(n, dz)
            for way in (0, 1):
                begin(b2(n, way, dz, mx))
        for half in (0, 1):
            b1_wait(n, 4, half=half)
        for way in (0, 1):
            begin(b2(n, way, 4, mx))

    order = (0, -1, 1, -2, 2, -3, 3, 4)

    def spread_across(n):
        for i, dz in enumerate(order):
            for way in (0, 1):
                source = x_of(2 * way - 1)
                b2(n, way, dz, source).wait_recv()
                if i % 2 == way:
                    begin(b3(n, way, dz, source))

    def spread_end(n):
        for i, dz in enumerate(order):
            b3(n, i % 2, dz, x_of(2)).wait_recv()

    def calibrate(n):
        @pl.loop(0, NX)
        def _(x):
            rows = pl.ds(pl.multiple_of(x * NZ * OWN, NZ * OWN), NZ * OWN)
            q = shared[n, x].reshape(NZ * OWN, 2 * APAD).astype(I32)
            for s in (0, 1):
                cols = slice(s * APAD, (s + 1) * APAD)
                part = q[:, cols]
                k = part[:, ANTENNA_COUNT:ANTENNA_COUNT + 1] - 15
                g = part.astype(F32) * jnp.exp2(k.astype(F32))
                high = g.astype(BF16)
                g_full[rows, cols] = g
                g_high[rows, cols] = high
                g_low[rows, cols] = (g - high.astype(F32)).astype(BF16)

        for s in (0, 1):
            cols = slice(s * APAD, (s + 1) * APAD)
            combo[s] = nt(select[s], g_high[:, cols]) + nt(select[s], g_low[:, cols])

        @pl.loop(1, NTA + 1)
        def _(j):
            d = time_peer(j)
            rows = pl.ds(pl.multiple_of(d * BASE, BASE), BASE)
            cols = slice(n * CW, (n + 1) * CW)
            u = amp[rows, cols].astype(F32) - combo[0, rows, :]
            v = ph[rows, cols].astype(F32) - combo[1, rows, :]
            magnitude = jnp.exp(u)
            sine, cosine = sin_cos(v)
            out_cal[n, d, 0] = (magnitude * cosine).astype(BF16)
            out_cal[n, d, 1] = (magnitude * sine).astype(BF16)

            @pl.when(j < NTA)
            def _():
                cal_copy(n, j).start()

        in_cal[n, 0] = out_cal[n, mt]
        for s in (0, 1):
            @pl.loop(0, CW // TILE)
            def _(k):
                block = g_full[pl.ds(pl.multiple_of(k * TILE, TILE), TILE), s * APAD:(s + 1) * APAD]
                start = s * ANTENNA_COUNT * NTILE + n * (CW // TILE) + k
                gains[pl.ds(start, ANTENNA_COUNT, stride=NTILE), :] = block.T[0:ANTENNA_COUNT]

    def mask(n):
        @pl.loop(0, NTA)
        def _(j):
            @pl.when(j > 0)
            def _():
                cal_copy(n, j).wait_recv()

            row = pl.multiple_of(lax.rem(mt - j + NTA, NTA) * LINE, LINE)
            w = keep[:, n * CW:(n + 1) * CW].astype(BF16)
            for c in (0, 1):
                masked[pl.ds(row + c * BASE, BASE), EDGE + n * CW:EDGE + (n + 1) * CW] = (
                    in_cal[n, j, c] * w
                )

    def fill(low, high):
        @pl.loop(low, high)
        def _(p):
            lane = pl.multiple_of(p * PAIR, PAIR)
            mixed[...] = nt(masked[:, pl.ds(lane, WINDOW)], wide[...])

            @pl.loop(0, NT)
            def _(to):
                total = times[to, 0]
                value = times[to, 0] * mixed[0:LINE]
                for t in range(1, NT):
                    total = total + times[to, t]
                    value = value + times[to, t] * mixed[t * LINE:(t + 1) * LINE]
                ratio = rden[:, pl.ds(lane, PAIR)] * (1.0 / jnp.full((1, PAIR), total, F32))
                w = keep[:, pl.ds(lane, PAIR)]
                for c in (0, 1):
                    row = pl.multiple_of(to * LINE + c * BASE, BASE)
                    own = masked[pl.ds(row, BASE), pl.ds(pl.multiple_of(lane + EDGE, TILE), PAIR)]
                    result = jnp.where(
                        w > 0.5, own.astype(F32), value[c * BASE:(c + 1) * BASE] * ratio
                    )
                    for i in (0, 1):
                        start = c * BASE * NTILE * NT + (2 * p + i) * NT + to
                        filled[pl.ds(start, BASE, stride=NTILE * NT), :] = (
                            result[:, i * TILE:(i + 1) * TILE]
                        )

    add_sums()
    solve()
    for n in range(PARTS):
        spread_start(n)
    spread_near(0)
    spread_near(1)
    spread_far(0)
    spread_near(2)
    spread_far(1)
    spread_across(0)
    spread_far(2)
    spread_across(1)
    spread_end(0)
    calibrate(0)
    spread_across(2)
    spread_end(1)
    calibrate(1)
    mask(0)
    mask(1)
    fill(0, 2)
    spread_end(2)
    calibrate(2)
    mask(2)
    fill(2, NTILE // 2)

    for copy in started:
        copy.wait_send()

    @pl.loop(1, NBL)
    def _(j):
        index_copy(j).wait_send()
        data_copy(j).wait_send()

    @pl.loop(1, NTA)
    def _(j):
        for n in range(PARTS):
            cal_copy(n, j).wait_send()


def calibrate_and_fill(amp, ph, group_row, couples, flags, times, channel, inverse):
    dma = pltpu.SemaphoreType.DMA
    vmem = pl.BlockSpec(memory_space=pltpu.VMEM)
    hbm = pl.BlockSpec(memory_space=pltpu.HBM)
    return pl.pallas_call(
        whole_kernel,
        name="calibrate_and_fill",
        out_shape=(
            jax.ShapeDtypeStruct((2 * ANTENNA_COUNT * NTILE, TILE), F32),
            jax.ShapeDtypeStruct((2 * BASE * NTILE * NT, TILE), F32),
        ),
        in_specs=[hbm] * 8,
        out_specs=(vmem, vmem),
        scratch_shapes=[
            pltpu.VMEM((ROWS, CH), BF16),
            pltpu.VMEM((ROWS, CH), BF16),
            pltpu.VMEM((1, ROWS), I32),
            pltpu.VMEM((2, ROWS), I32),
            pltpu.VMEM((NTILE, BASE), I32),
            pltpu.SMEM((NT, NT), F32),
            pltpu.VMEM((2 * REACH + 1, TILE, TILE), BF16),
            pltpu.VMEM((ANTENNA_COUNT, 2, ANTENNA_COUNT), F32),
            dma((8,)),
            pltpu.VMEM((NBL, 2 * MINE, ROWS), BF16),
            pltpu.VMEM((NBL, 2 * MINE, ROWS), BF16),
            pltpu.VMEM((8, 128), I16),
            pltpu.VMEM((NBL, 8, 128), I16),
            pltpu.VMEM((2, APAD, A8), F32),
            pltpu.VMEM((HOT, NGRP + 2 * MINE), F32),
            pltpu.VMEM((PARTS, NX, NZ, OWN, 2 * APAD), I16),
            pltpu.VMEM((CW, 2 * APAD), F32),
            pltpu.VMEM((CW, 2 * APAD), BF16),
            pltpu.VMEM((CW, 2 * APAD), BF16),
            pltpu.VMEM((2, ROWS, APAD), BF16),
            pltpu.VMEM((2, ROWS, CW), F32),
            pltpu.VMEM((PAIR, WINDOW), BF16),
            pltpu.VMEM((BASE, CH), F32),
            pltpu.VMEM((BASE, CH + 2 * EDGE), BF16),
            pltpu.VMEM((NT * LINE, CH + 2 * EDGE), BF16),
            pltpu.VMEM((BASE, CH), F32),
            pltpu.VMEM((NT * LINE, PAIR), F32),
            pltpu.VMEM((PARTS, NTA, 2, BASE, CW), BF16),
            pltpu.VMEM((PARTS, NTA, 2, BASE, CW), BF16),
            dma((NBL,)), dma((NBL,)), dma((NBL,)), dma((NBL,)),
            dma((PARTS, NZ)), dma((PARTS, NZ)), dma((PARTS, 2, NZ)), dma((PARTS, 2, NZ)),
            dma((PARTS, NZ)), dma((PARTS, NZ)), dma((PARTS, NTA)), dma((PARTS, NTA)),
        ],
        compiler_params=pltpu.CompilerParams(
            collective_id=0, has_side_effects=True, vmem_limit_bytes=40 * 2**20
        ),
    )(*(
        pltpu.with_memory_space_constraint(x, pltpu.HBM)
        for x in (amp, ph, group_row, couples, flags, times, channel, inverse)
    ))


def copy_kernel(a, b, out_a, out_b, sem):
    copies = []
    for k, (src, dst) in enumerate(((a, out_a), (b, out_b))):
        size = src.shape[0] // 2
        for i in range(2):
            rows = pl.ds(i * size, size)
            copies.append(pltpu.make_async_copy(src.at[rows], dst.at[rows], sem.at[k, i]))
    for copy in copies:
        copy.start()
    for copy in copies:
        copy.wait()


def copy_out(a, b):
    return pl.pallas_call(
        copy_kernel,
        name="copy_out",
        out_shape=(
            jax.ShapeDtypeStruct(a.shape, a.dtype), jax.ShapeDtypeStruct(b.shape, b.dtype)
        ),
        in_specs=[pl.BlockSpec(memory_space=pltpu.VMEM)] * 2,
        out_specs=(pl.BlockSpec(memory_space=pl.ANY),) * 2,
        scratch_shapes=[pltpu.SemaphoreType.DMA((2, 2))],
        compiler_params=pltpu.CompilerParams(vmem_limit_bytes=10 * 2**20),
    )(a, b)


def on_device(
    log_amplitude,
    phase,
    redundant_group_index,
    antenna_couples,
    tile_flag_mask,
    inverse,
    integration_kernel,
    channel_kernel,
):
    gains, filled = copy_out(*calibrate_and_fill(
        log_amplitude[:, 0], phase[:, 0], redundant_group_index[None, :], antenna_couples.T,
        tile_flag_mask.T, integration_kernel, channel_kernel, inverse.transpose(1, 0, 2),
    ))
    return (
        gains.reshape(2, ANTENNA_COUNT, 1, CH),
        filled.reshape(2, BASE, NTILE, NT, TILE).transpose(0, 1, 3, 2, 4).reshape(2, BASE, NT, CH),
    )


def solution(mesh):
    in_specs = (
        P("bl", "ta", None),
        P("bl", "ta", None),
        P("bl"),
        P("bl", None),
        P(("bl", "ta"), None),
        P(),
        P(),
        P(),
    )
    out_specs = (P(None, None, "ta", None), P(None, ("bl", "ta"), None, None))
    return jax.shard_map(
        on_device, mesh=mesh, in_specs=in_specs, out_specs=out_specs, check_vma=False
    )
```

```python
import jax
import jax.numpy as jnp
from jax import lax
from jax.experimental import pallas as pl
from jax.experimental.pallas import tpu as pltpu
from jax.sharding import PartitionSpec as P

ANTENNA_COUNT = 350
NGRP = 224
TILE = 128
REACH = 3
HIGH = lax.Precision.HIGHEST
F32 = jnp.float32
BF16 = jnp.bfloat16
I16 = jnp.int16
I32 = jnp.int32
MESH = pl.DeviceIdType.MESH

NX, NZ = 4, 8
NBL = NX * NZ
NTA = 8
NT = 8
ROWS = 256
BASE = ROWS // NTA
CH = 1536
PARTS = 3
CW = CH // PARTS
OWN = CW // NBL
APAD = 384
A8 = 352
HOT = NGRP + 2 * A8
NTILE = CH // TILE
PAIR = 2 * TILE
WINDOW = 8 * TILE
EDGE = REACH * TILE
LINE = 2 * BASE
MINE = PARTS * OWN


def nt(a, b, precision=None):
    return lax.dot_general(
        a, b, (((1,), (1,)), ((), ())), preferred_element_type=F32, precision=precision
    )


def encode(g):
    peak = jnp.max(jnp.abs(g), axis=1, keepdims=True)
    k = jnp.floor(jnp.log2(jnp.maximum(peak, F32(2.0**-100)))).astype(I32) + 2
    coded = jnp.round(g * jnp.exp2((15 - k).astype(F32))).astype(I32)
    lane = lax.broadcasted_iota(I32, g.shape, 1)
    return jnp.where(lane == ANTENNA_COUNT, k, coded)


def sin_cos(v):
    n = jnp.round(v * F32(0.6366197723675814))
    r = v - n * F32(1.5703125)
    r = r - n * F32(4.837512969970703125e-4)
    r = r - n * F32(7.54978995489188216e-8)
    quadrant = n.astype(I32)
    z = r * r
    s = ((F32(-1.9515295891e-4) * z + F32(8.3321608736e-3)) * z - F32(1.6666654611e-1)) * z * r + r
    c = (
        (F32(2.443315711809948e-5) * z - F32(1.388731625493765e-3)) * z + F32(4.166664568298827e-2)
    ) * z * z - F32(0.5) * z + F32(1.0)
    swap = (quadrant & 1) != 0
    sine = jnp.where(swap, c, s)
    cosine = jnp.where(swap, s, c)
    sine = jnp.where((quadrant & 2) != 0, -sine, sine)
    cosine = jnp.where(((quadrant + 1) & 2) != 0, -cosine, cosine)
    return sine, cosine


def whole_kernel(
    amp_in, ph_in, group_in, couples_in, flags_in, times_in, channel_in, inverse_in, gains, filled,
    amp, ph, group_row, couples, flags, times, channel, inverse, in_sem, send, got, index, got_index, inv, total, shared,
    g_full, g_high, g_low, select, combo, wide, keep, keep_wide, masked, rden, mixed,
    out_cal, in_cal,
    index_send, index_recv, data_send, data_recv, b1_send, b1_recv, b2_send, b2_recv,
    b3_send, b3_recv, cal_send, cal_recv,
):
    me = lax.axis_index("bl")
    mx, mz = me // NZ, lax.rem(me, NZ)
    mt = lax.axis_index("ta")

    def x_of(dx):
        return lax.rem(mx + dx + NX, NX)

    def z_of(dz):
        return lax.rem(mz + dz + NZ, NZ)

    def device(dx, dz):
        return x_of(dx) * NZ + z_of(dz)

    def peer_of(j):
        return device(j // NZ, lax.rem(3 * j, NZ))

    def time_peer(j):
        return lax.rem(mt + j, NTA)

    def remote(src, dst, send_sem, recv_sem, axis, peer):
        return pltpu.make_async_remote_copy(
            src_ref=src, dst_ref=dst, send_sem=send_sem, recv_sem=recv_sem,
            device_id={axis: peer}, device_id_type=MESH,
        )

    def index_copy(j):
        return remote(
            index, got_index.at[j], index_send.at[j], index_recv.at[j], "bl", peer_of(j)
        )

    def data_copy(j):
        peer = peer_of(j)
        return remote(send.at[peer], got.at[j], data_send.at[j], data_recv.at[j], "bl", peer)

    def cal_copy(n, j):
        peer = time_peer(j)
        return remote(
            out_cal.at[n, peer], in_cal.at[n, j], cal_send.at[n, j], cal_recv.at[n, j], "ta", peer
        )

    def b1(n, dz, step, half=None):
        slot = shared.at[n, mx, z_of(dz)]
        number = (step - dz) % NZ
        if half is not None:
            slot = slot.at[:, pl.ds(half * APAD, APAD)]
            number = 4 * half
        return remote(slot, slot, b1_send.at[n, number], b1_recv.at[n, number], "bl", device(0, step))

    def b1_wait(n, dz, half=None):
        slot = shared.at[n, mx, z_of(dz)]
        number = (-dz) % NZ
        if half is not None:
            slot = slot.at[:, pl.ds(half * APAD, APAD)]
            number = 4 * half
        remote(slot, slot, b1_send.at[n, number], b1_recv.at[n, number], "bl", device(0, 1)).wait_recv()

    def b2(n, way, dz, src_x):
        slot = shared.at[n, src_x, z_of(dz)]
        number = dz % NZ
        return remote(
            slot, slot, b2_send.at[n, way, number], b2_recv.at[n, way, number],
            "bl", device(1 - 2 * way, 0),
        )

    def b3(n, way, dz, src_x):
        slot = shared.at[n, src_x, z_of(dz)]
        number = dz % NZ
        return remote(
            slot, slot, b3_send.at[n, number], b3_recv.at[n, number], "bl", device(1 - 2 * way, 0)
        )

    incoming = [
        pltpu.make_async_copy(src, dst, in_sem.at[k])
        for k, (src, dst) in enumerate((
            (amp_in, amp), (ph_in, ph), (group_in, group_row), (couples_in, couples),
            (flags_in, flags), (times_in, times), (channel_in, channel), (inverse_in, inverse),
        ))
    ]
    for copy in incoming:
        copy.start()
    barrier = pltpu.get_barrier_semaphore()

    @pl.loop(1, NBL)
    def _(j):
        pl.semaphore_signal(barrier, inc=1, device_id={"bl": peer_of(j)}, device_id_type=MESH)

    @pl.loop(1, NTA)
    def _(j):
        pl.semaphore_signal(barrier, inc=1, device_id={"ta": time_peer(j)}, device_id_type=MESH)

    def turn(n):
        cols = slice(n * CW, (n + 1) * CW)
        for s, ref in enumerate((amp, ph)):
            first = s * MINE + n * OWN
            send[:, first:first + OWN, :] = ref[:, cols].T.reshape(NBL, OWN, ROWS)

    for copy in incoming[:4]:
        copy.wait()
    index[...] = jnp.concatenate(
        [
            ref[k:k + 1, h * TILE:(h + 1) * TILE]
            for ref, k in ((group_row, 0), (couples, 0), (couples, 1)) for h in (0, 1)
        ] + [jnp.zeros((2, TILE), I32)], axis=0
    ).astype(I16)
    for n in range(PARTS):
        turn(n)
    pl.semaphore_wait(barrier, NBL - 1 + NTA - 1)

    @pl.loop(1, NBL)
    def _(j):
        index_copy(j).start()

    @pl.loop(1, NBL)
    def _(j):
        data_copy(j).start()

    for copy in incoming[4:]:
        copy.wait()
    got[0] = send[me]
    got_index[0] = index[...]
    inv[...] = jnp.zeros_like(inv)
    for s in (0, 1):
        inv[s, 0:ANTENNA_COUNT, 0:ANTENNA_COUNT] = inverse[:, s, :]
    label = lax.broadcasted_iota(I32, (APAD, ROWS), 0)
    first = (couples[0:1, :] == label).astype(F32)
    second = (couples[1:2, :] == label).astype(F32)
    select[0] = (first + second).T.astype(BF16)
    select[1] = (first - second).T.astype(BF16)
    wide[...] = jnp.zeros_like(wide)
    for c in (0, 1):
        for o in range(2 * REACH + 1):
            wide[c * TILE:(c + 1) * TILE, (c + o) * TILE:(c + o + 1) * TILE] = channel[o]
    masked[...] = jnp.zeros_like(masked)
    keep_wide[...] = jnp.zeros_like(keep_wide)
    tile = lax.broadcasted_iota(I32, (NTILE, CH), 1) // TILE
    spread = (tile == lax.broadcasted_iota(I32, (NTILE, CH), 0)).astype(F32).astype(BF16)
    open_tiles = (1 - flags[...]).astype(F32).astype(BF16)
    keep[...] = lax.dot_general(
        open_tiles, spread, (((0,), (0,)), ((), ())), preferred_element_type=F32
    )
    keep_wide[:, EDGE:EDGE + CH] = keep[...].astype(BF16)
    for p in range(NTILE // 2):
        rden[:, PAIR * p:PAIR * (p + 1)] = 1.0 / nt(
            keep_wide[:, PAIR * p:PAIR * p + WINDOW], wide[...]
        )

    def clear(*refs):
        for ref in refs:
            ref[...] = jnp.zeros_like(ref)

    clear(total)

    def add_sums():
        @pl.loop(0, NBL)
        def _(j):
            @pl.when(j > 0)
            def _():
                index_copy(j).wait_recv()
                data_copy(j).wait_recv()

            ix = got_index[j].astype(I32)

            def one_hot(k, size):
                row = jnp.concatenate([ix[2 * k:2 * k + 1], ix[2 * k + 1:2 * k + 2]], axis=1)
                return (lax.broadcasted_iota(I32, (size, ROWS), 0) == row).astype(F32)

            group = one_hot(0, NGRP).astype(BF16)
            one, two = one_hot(1, A8), one_hot(2, A8)
            hot = jnp.concatenate(
                [group, (one + two).astype(BF16), (one - two).astype(BF16)], axis=0
            )
            total[...] += nt(hot, jnp.concatenate([group, got[j]], axis=0))

    def solve():
        count = jnp.sum(total[0:NGRP, 0:NGRP], axis=1, keepdims=True)
        mean = total[0:NGRP, NGRP:NGRP + 2 * MINE] / count
        for s in (0, 1):
            rows = slice(NGRP + s * A8, NGRP + (s + 1) * A8)
            cols = slice(s * MINE, (s + 1) * MINE)
            rhs = total[rows, NGRP + s * MINE:NGRP + (s + 1) * MINE] - jnp.dot(
                total[rows, 0:NGRP], mean[:, cols], precision=HIGH, preferred_element_type=F32
            )
            coded = encode(nt(rhs.T, inv[s], HIGH)).astype(I16)
            for n in range(PARTS):
                shared[n, mx, mz, :, s * APAD:(s + 1) * APAD] = coded[n * OWN:(n + 1) * OWN]

    started = []

    def begin(copy):
        copy.start()
        started.append(copy)

    def spread_start(n):
        for step in (1, -1, 2, -2):
            begin(b1(n, 0, step))
        for way in (0, 1):
            begin(b2(n, way, 0, mx))

    def spread_near(n):
        for sign in (-1, 1):
            b1_wait(n, sign)
            for way in (0, 1):
                begin(b2(n, way, sign, mx))
        for sign in (-1, 1):
            b1_wait(n, 2 * sign)
            begin(b1(n, 2 * sign, -sign))
            begin(b1(n, 2 * sign, -2 * sign, half=0 if sign < 0 else 1))
            for way in (0, 1):
                begin(b2(n, way, 2 * sign, mx))

    def spread_far(n):
        for dz in (-3, 3):
            b1_wait(n, dz)
            for way in (0, 1):
                begin(b2(n, way, dz, mx))
        for half in (0, 1):
            b1_wait(n, 4, half=half)
        for way in (0, 1):
            begin(b2(n, way, 4, mx))

    order = (0, -1, 1, -2, 2, -3, 3, 4)

    def spread_across(n):
        for i, dz in enumerate(order):
            for way in (0, 1):
                source = x_of(2 * way - 1)
                b2(n, way, dz, source).wait_recv()
                if i % 2 == way:
                    begin(b3(n, way, dz, source))

    def spread_end(n):
        for i, dz in enumerate(order):
            b3(n, i % 2, dz, x_of(2)).wait_recv()

    def calibrate(n):
        @pl.loop(0, NX)
        def _(x):
            rows = pl.ds(pl.multiple_of(x * NZ * OWN, NZ * OWN), NZ * OWN)
            q = shared[n, x].reshape(NZ * OWN, 2 * APAD).astype(I32)
            for s in (0, 1):
                cols = slice(s * APAD, (s + 1) * APAD)
                part = q[:, cols]
                k = part[:, ANTENNA_COUNT:ANTENNA_COUNT + 1] - 15
                g = part.astype(F32) * jnp.exp2(k.astype(F32))
                high = g.astype(BF16)
                g_full[n, rows, cols] = g
                g_high[rows, cols] = high
                g_low[rows, cols] = (g - high.astype(F32)).astype(BF16)

        for s in (0, 1):
            cols = slice(s * APAD, (s + 1) * APAD)
            combo[s] = nt(select[s], g_high[:, cols]) + nt(select[s], g_low[:, cols])

        @pl.loop(1, NTA + 1)
        def _(j):
            d = time_peer(j)
            rows = pl.ds(pl.multiple_of(d * BASE, BASE), BASE)
            cols = slice(n * CW, (n + 1) * CW)
            u = amp[rows, cols].astype(F32) - combo[0, rows, :]
            v = ph[rows, cols].astype(F32) - combo[1, rows, :]
            magnitude = jnp.exp(u)
            sine, cosine = sin_cos(v)
            out_cal[n, d, 0] = (magnitude * cosine).astype(BF16)
            out_cal[n, d, 1] = (magnitude * sine).astype(BF16)

            @pl.when(j < NTA)
            def _():
                cal_copy(n, j).start()

        in_cal[n, 0] = out_cal[n, mt]

    def write_gains(n):
        for s in (0, 1):
            @pl.loop(0, CW // TILE)
            def _(k):
                rows = pl.ds(pl.multiple_of(k * TILE, TILE), TILE)
                block = g_full[n, rows, s * APAD:(s + 1) * APAD]
                start = s * ANTENNA_COUNT * NTILE + n * (CW // TILE) + k
                gains[pl.ds(start, ANTENNA_COUNT, stride=NTILE), :] = block.T[0:ANTENNA_COUNT]

    def mask(n):
        @pl.loop(0, NTA)
        def _(j):
            @pl.when(j > 0)
            def _():
                cal_copy(n, j).wait_recv()

            row = pl.multiple_of(lax.rem(mt - j + NTA, NTA) * LINE, LINE)
            w = keep[:, n * CW:(n + 1) * CW].astype(BF16)
            for c in (0, 1):
                masked[pl.ds(row + c * BASE, BASE), EDGE + n * CW:EDGE + (n + 1) * CW] = (
                    in_cal[n, j, c] * w
                )

    def fill(low, high):
        @pl.loop(low, high)
        def _(p):
            lane = pl.multiple_of(p * PAIR, PAIR)
            mixed[...] = nt(masked[:, pl.ds(lane, WINDOW)], wide[...])

            @pl.loop(0, NT)
            def _(to):
                total = times[to, 0]
                value = times[to, 0] * mixed[0:LINE]
                for t in range(1, NT):
                    total = total + times[to, t]
                    value = value + times[to, t] * mixed[t * LINE:(t + 1) * LINE]
                ratio = rden[:, pl.ds(lane, PAIR)] * (1.0 / jnp.full((1, PAIR), total, F32))
                w = keep[:, pl.ds(lane, PAIR)]
                for c in (0, 1):
                    row = pl.multiple_of(to * LINE + c * BASE, BASE)
                    own = masked[pl.ds(row, BASE), pl.ds(pl.multiple_of(lane + EDGE, TILE), PAIR)]
                    result = jnp.where(
                        w > 0.5, own.astype(F32), value[c * BASE:(c + 1) * BASE] * ratio
                    )
                    for i in (0, 1):
                        start = c * BASE * NTILE * NT + (2 * p + i) * NT + to
                        filled[pl.ds(start, BASE, stride=NTILE * NT), :] = (
                            result[:, i * TILE:(i + 1) * TILE]
                        )

    add_sums()
    solve()
    for n in range(PARTS):
        spread_start(n)
    spread_near(0)
    spread_near(1)
    spread_far(0)
    spread_near(2)
    spread_far(1)
    spread_across(0)
    spread_far(2)
    spread_across(1)
    spread_end(0)
    calibrate(0)
    spread_across(2)
    spread_end(1)
    calibrate(1)
    spread_end(2)
    calibrate(2)
    write_gains(0)
    mask(0)
    write_gains(1)
    mask(1)
    fill(0, 2)
    write_gains(2)
    mask(2)
    fill(2, NTILE // 2)

    for copy in started:
        copy.wait_send()

    @pl.loop(1, NBL)
    def _(j):
        index_copy(j).wait_send()
        data_copy(j).wait_send()

    @pl.loop(1, NTA)
    def _(j):
        for n in range(PARTS):
            cal_copy(n, j).wait_send()


def calibrate_and_fill(amp, ph, group_row, couples, flags, times, channel, inverse):
    dma = pltpu.SemaphoreType.DMA
    vmem = pl.BlockSpec(memory_space=pltpu.VMEM)
    hbm = pl.BlockSpec(memory_space=pltpu.HBM)
    return pl.pallas_call(
        whole_kernel,
        name="calibrate_and_fill",
        out_shape=(
            jax.ShapeDtypeStruct((2 * ANTENNA_COUNT * NTILE, TILE), F32),
            jax.ShapeDtypeStruct((2 * BASE * NTILE * NT, TILE), F32),
        ),
        in_specs=[hbm] * 8,
        out_specs=(vmem, vmem),
        scratch_shapes=[
            pltpu.VMEM((ROWS, CH), BF16),
            pltpu.VMEM((ROWS, CH), BF16),
            pltpu.VMEM((1, ROWS), I32),
            pltpu.VMEM((2, ROWS), I32),
            pltpu.VMEM((NTILE, BASE), I32),
            pltpu.SMEM((NT, NT), F32),
            pltpu.VMEM((2 * REACH + 1, TILE, TILE), BF16),
            pltpu.VMEM((ANTENNA_COUNT, 2, ANTENNA_COUNT), F32),
            dma((8,)),
            pltpu.VMEM((NBL, 2 * MINE, ROWS), BF16),
            pltpu.VMEM((NBL, 2 * MINE, ROWS), BF16),
            pltpu.VMEM((8, 128), I16),
            pltpu.VMEM((NBL, 8, 128), I16),
            pltpu.VMEM((2, APAD, A8), F32),
            pltpu.VMEM((HOT, NGRP + 2 * MINE), F32),
            pltpu.VMEM((PARTS, NX, NZ, OWN, 2 * APAD), I16),
            pltpu.VMEM((PARTS, CW, 2 * APAD), F32),
            pltpu.VMEM((CW, 2 * APAD), BF16),
            pltpu.VMEM((CW, 2 * APAD), BF16),
            pltpu.VMEM((2, ROWS, APAD), BF16),
            pltpu.VMEM((2, ROWS, CW), F32),
            pltpu.VMEM((PAIR, WINDOW), BF16),
            pltpu.VMEM((BASE, CH), F32),
            pltpu.VMEM((BASE, CH + 2 * EDGE), BF16),
            pltpu.VMEM((NT * LINE, CH + 2 * EDGE), BF16),
            pltpu.VMEM((BASE, CH), F32),
            pltpu.VMEM((NT * LINE, PAIR), F32),
            pltpu.VMEM((PARTS, NTA, 2, BASE, CW), BF16),
            pltpu.VMEM((PARTS, NTA, 2, BASE, CW), BF16),
            dma((NBL,)), dma((NBL,)), dma((NBL,)), dma((NBL,)),
            dma((PARTS, NZ)), dma((PARTS, NZ)), dma((PARTS, 2, NZ)), dma((PARTS, 2, NZ)),
            dma((PARTS, NZ)), dma((PARTS, NZ)), dma((PARTS, NTA)), dma((PARTS, NTA)),
        ],
        compiler_params=pltpu.CompilerParams(
            collective_id=0, has_side_effects=True, vmem_limit_bytes=40 * 2**20
        ),
    )(*(
        pltpu.with_memory_space_constraint(x, pltpu.HBM)
        for x in (amp, ph, group_row, couples, flags, times, channel, inverse)
    ))


def copy_kernel(a, b, out_a, out_b, sem):
    copies = []
    for k, (src, dst) in enumerate(((a, out_a), (b, out_b))):
        size = src.shape[0] // 2
        for i in range(2):
            rows = pl.ds(i * size, size)
            copies.append(pltpu.make_async_copy(src.at[rows], dst.at[rows], sem.at[k, i]))
    for copy in copies:
        copy.start()
    for copy in copies:
        copy.wait()


def copy_out(a, b):
    return pl.pallas_call(
        copy_kernel,
        name="copy_out",
        out_shape=(
            jax.ShapeDtypeStruct(a.shape, a.dtype), jax.ShapeDtypeStruct(b.shape, b.dtype)
        ),
        in_specs=[pl.BlockSpec(memory_space=pltpu.VMEM)] * 2,
        out_specs=(pl.BlockSpec(memory_space=pl.ANY),) * 2,
        scratch_shapes=[pltpu.SemaphoreType.DMA((2, 2))],
        compiler_params=pltpu.CompilerParams(vmem_limit_bytes=10 * 2**20),
    )(a, b)


def on_device(
    log_amplitude,
    phase,
    redundant_group_index,
    antenna_couples,
    tile_flag_mask,
    inverse,
    integration_kernel,
    channel_kernel,
):
    gains, filled = copy_out(*calibrate_and_fill(
        log_amplitude[:, 0], phase[:, 0], redundant_group_index[None, :], antenna_couples.T,
        tile_flag_mask.T, integration_kernel, channel_kernel, inverse.transpose(1, 0, 2),
    ))
    return (
        gains.reshape(2, ANTENNA_COUNT, 1, CH),
        filled.reshape(2, BASE, NTILE, NT, TILE).transpose(0, 1, 3, 2, 4).reshape(2, BASE, NT, CH),
    )


def solution(mesh):
    in_specs = (
        P("bl", "ta", None),
        P("bl", "ta", None),
        P("bl"),
        P("bl", None),
        P(("bl", "ta"), None),
        P(),
        P(),
        P(),
    )
    out_specs = (P(None, None, "ta", None), P(None, ("bl", "ta"), None, None))
    return jax.shard_map(
        on_device, mesh=mesh, in_specs=in_specs, out_specs=out_specs, check_vma=False
    )
```

```python
import jax
import jax.numpy as jnp
from jax import lax
from jax.experimental import pallas as pl
from jax.experimental.pallas import tpu as pltpu
from jax.sharding import PartitionSpec as P

ANTENNA_COUNT = 350
NGRP = 224
TILE = 128
REACH = 3
HIGH = lax.Precision.HIGHEST
F32 = jnp.float32
BF16 = jnp.bfloat16
I16 = jnp.int16
I32 = jnp.int32
MESH = pl.DeviceIdType.MESH

NX, NZ = 4, 8
NBL = NX * NZ
NTA = 8
NT = 8
ROWS = 256
BASE = ROWS // NTA
CH = 1536
PARTS = 3
CW = CH // PARTS
OWN = CW // NBL
APAD = 384
A8 = 352
HOT = NGRP + 2 * A8
NTILE = CH // TILE
PAIR = 2 * TILE
WINDOW = 8 * TILE
EDGE = REACH * TILE
LINE = 2 * BASE
MINE = PARTS * OWN


def nt(a, b, precision=None):
    return lax.dot_general(
        a, b, (((1,), (1,)), ((), ())), preferred_element_type=F32, precision=precision
    )


def encode(g):
    peak = jnp.max(jnp.abs(g), axis=1, keepdims=True)
    k = jnp.floor(jnp.log2(jnp.maximum(peak, F32(2.0**-100)))).astype(I32) + 2
    coded = jnp.round(g * jnp.exp2((15 - k).astype(F32))).astype(I32)
    lane = lax.broadcasted_iota(I32, g.shape, 1)
    return jnp.where(lane == ANTENNA_COUNT, k, coded)


def sin_cos(v):
    n = jnp.round(v * F32(0.6366197723675814))
    r = v - n * F32(1.5703125)
    r = r - n * F32(4.837512969970703125e-4)
    r = r - n * F32(7.54978995489188216e-8)
    quadrant = n.astype(I32)
    z = r * r
    s = ((F32(-1.9515295891e-4) * z + F32(8.3321608736e-3)) * z - F32(1.6666654611e-1)) * z * r + r
    c = (
        (F32(2.443315711809948e-5) * z - F32(1.388731625493765e-3)) * z + F32(4.166664568298827e-2)
    ) * z * z - F32(0.5) * z + F32(1.0)
    swap = (quadrant & 1) != 0
    sine = jnp.where(swap, c, s)
    cosine = jnp.where(swap, s, c)
    sine = jnp.where((quadrant & 2) != 0, -sine, sine)
    cosine = jnp.where(((quadrant + 1) & 2) != 0, -cosine, cosine)
    return sine, cosine


def whole_kernel(
    amp_in, ph_in, group_in, couples_in, flags_in, times_in, channel_in, inverse_in, gains, filled,
    amp, ph, group_row, couples, flags, times, channel, inverse, in_sem, send, got, index, got_index, inv, total, shared,
    g_full, g_high, g_low, select, combo, wide, keep, keep_wide, masked, rden, mixed,
    early, out_cal, in_cal,
    index_send, index_recv, data_send, data_recv, b1_send, b1_recv, b2_send, b2_recv,
    b3_send, b3_recv, cal_send, cal_recv,
):
    me = lax.axis_index("bl")
    mx, mz = me // NZ, lax.rem(me, NZ)
    mt = lax.axis_index("ta")

    def x_of(dx):
        return lax.rem(mx + dx + NX, NX)

    def z_of(dz):
        return lax.rem(mz + dz + NZ, NZ)

    def device(dx, dz):
        return x_of(dx) * NZ + z_of(dz)

    def peer_of(j):
        return device(j // NZ, lax.rem(3 * j, NZ))

    def time_peer(j):
        return lax.rem(mt + j, NTA)

    def remote(src, dst, send_sem, recv_sem, axis, peer):
        return pltpu.make_async_remote_copy(
            src_ref=src, dst_ref=dst, send_sem=send_sem, recv_sem=recv_sem,
            device_id={axis: peer}, device_id_type=MESH,
        )

    def index_copy(j):
        return remote(
            index, got_index.at[j], index_send.at[j], index_recv.at[j], "bl", peer_of(j)
        )

    def data_copy(j):
        peer = peer_of(j)
        return remote(send.at[peer], got.at[j], data_send.at[j], data_recv.at[j], "bl", peer)

    def cal_copy(n, j):
        peer = time_peer(j)
        return remote(
            out_cal.at[n, peer], in_cal.at[n, j], cal_send.at[n, j], cal_recv.at[n, j], "ta", peer
        )

    def b1(n, dz, step, half=None):
        slot = shared.at[n, mx, z_of(dz)]
        number = (step - dz) % NZ
        if half is not None:
            slot = slot.at[:, pl.ds(half * APAD, APAD)]
            number = 4 * half
        return remote(slot, slot, b1_send.at[n, number], b1_recv.at[n, number], "bl", device(0, step))

    def b1_wait(n, dz, half=None):
        slot = shared.at[n, mx, z_of(dz)]
        number = (-dz) % NZ
        if half is not None:
            slot = slot.at[:, pl.ds(half * APAD, APAD)]
            number = 4 * half
        remote(slot, slot, b1_send.at[n, number], b1_recv.at[n, number], "bl", device(0, 1)).wait_recv()

    def b2(n, way, dz, src_x):
        slot = shared.at[n, src_x, z_of(dz)]
        number = dz % NZ
        return remote(
            slot, slot, b2_send.at[n, way, number], b2_recv.at[n, way, number],
            "bl", device(1 - 2 * way, 0),
        )

    def b3(n, way, dz, src_x):
        slot = shared.at[n, src_x, z_of(dz)]
        number = dz % NZ
        return remote(
            slot, slot, b3_send.at[n, number], b3_recv.at[n, number], "bl", device(1 - 2 * way, 0)
        )

    incoming = [
        pltpu.make_async_copy(src, dst, in_sem.at[k])
        for k, (src, dst) in enumerate((
            (amp_in, amp), (ph_in, ph), (group_in, group_row), (couples_in, couples),
            (flags_in, flags), (times_in, times), (channel_in, channel), (inverse_in, inverse),
        ))
    ]
    for copy in incoming:
        copy.start()
    barrier = pltpu.get_barrier_semaphore()

    @pl.loop(1, NBL)
    def _(j):
        pl.semaphore_signal(barrier, inc=1, device_id={"bl": peer_of(j)}, device_id_type=MESH)

    @pl.loop(1, NTA)
    def _(j):
        pl.semaphore_signal(barrier, inc=1, device_id={"ta": time_peer(j)}, device_id_type=MESH)

    def turn(n):
        cols = slice(n * CW, (n + 1) * CW)
        for s, ref in enumerate((amp, ph)):
            first = s * MINE + n * OWN
            send[:, first:first + OWN, :] = ref[:, cols].T.reshape(NBL, OWN, ROWS)

    for copy in incoming[:4]:
        copy.wait()
    index[...] = jnp.concatenate(
        [
            ref[k:k + 1, h * TILE:(h + 1) * TILE]
            for ref, k in ((group_row, 0), (couples, 0), (couples, 1)) for h in (0, 1)
        ] + [jnp.zeros((2, TILE), I32)], axis=0
    ).astype(I16)
    for n in range(PARTS):
        turn(n)
    pl.semaphore_wait(barrier, NBL - 1 + NTA - 1)

    @pl.loop(1, NBL)
    def _(j):
        index_copy(j).start()

    @pl.loop(1, NBL)
    def _(j):
        data_copy(j).start()

    for copy in incoming[4:]:
        copy.wait()
    got[0] = send[me]
    got_index[0] = index[...]
    inv[...] = jnp.zeros_like(inv)
    for s in (0, 1):
        inv[s, 0:ANTENNA_COUNT, 0:ANTENNA_COUNT] = inverse[:, s, :]
    label = lax.broadcasted_iota(I32, (APAD, ROWS), 0)
    first = (couples[0:1, :] == label).astype(F32)
    second = (couples[1:2, :] == label).astype(F32)
    select[0] = (first + second).T.astype(BF16)
    select[1] = (first - second).T.astype(BF16)
    wide[...] = jnp.zeros_like(wide)
    for c in (0, 1):
        for o in range(2 * REACH + 1):
            wide[c * TILE:(c + 1) * TILE, (c + o) * TILE:(c + o + 1) * TILE] = channel[o]
    masked[...] = jnp.zeros_like(masked)
    keep_wide[...] = jnp.zeros_like(keep_wide)
    tile = lax.broadcasted_iota(I32, (NTILE, CH), 1) // TILE
    spread = (tile == lax.broadcasted_iota(I32, (NTILE, CH), 0)).astype(F32).astype(BF16)
    open_tiles = (1 - flags[...]).astype(F32).astype(BF16)
    keep[...] = lax.dot_general(
        open_tiles, spread, (((0,), (0,)), ((), ())), preferred_element_type=F32
    )
    keep_wide[:, EDGE:EDGE + CH] = keep[...].astype(BF16)
    for p in range(NTILE // 2):
        rden[:, PAIR * p:PAIR * (p + 1)] = 1.0 / nt(
            keep_wide[:, PAIR * p:PAIR * p + WINDOW], wide[...]
        )

    def clear(*refs):
        for ref in refs:
            ref[...] = jnp.zeros_like(ref)

    clear(total)

    def add_sums():
        @pl.loop(0, NBL)
        def _(j):
            @pl.when(j > 0)
            def _():
                index_copy(j).wait_recv()
                data_copy(j).wait_recv()

            ix = got_index[j].astype(I32)

            def one_hot(k, size):
                row = jnp.concatenate([ix[2 * k:2 * k + 1], ix[2 * k + 1:2 * k + 2]], axis=1)
                return (lax.broadcasted_iota(I32, (size, ROWS), 0) == row).astype(F32)

            group = one_hot(0, NGRP).astype(BF16)
            one, two = one_hot(1, A8), one_hot(2, A8)
            hot = jnp.concatenate(
                [group, (one + two).astype(BF16), (one - two).astype(BF16)], axis=0
            )
            total[...] += nt(hot, jnp.concatenate([group, got[j]], axis=0))

    def solve():
        count = jnp.sum(total[0:NGRP, 0:NGRP], axis=1, keepdims=True)
        mean = total[0:NGRP, NGRP:NGRP + 2 * MINE] / count
        for s in (0, 1):
            rows = slice(NGRP + s * A8, NGRP + (s + 1) * A8)
            cols = slice(s * MINE, (s + 1) * MINE)
            rhs = total[rows, NGRP + s * MINE:NGRP + (s + 1) * MINE] - jnp.dot(
                total[rows, 0:NGRP], mean[:, cols], precision=HIGH, preferred_element_type=F32
            )
            coded = encode(nt(rhs.T, inv[s], HIGH)).astype(I16)
            for n in range(PARTS):
                shared[n, mx, mz, :, s * APAD:(s + 1) * APAD] = coded[n * OWN:(n + 1) * OWN]

    started = []

    def begin(copy):
        copy.start()
        started.append(copy)

    def spread_start(n):
        for step in (1, -1, 2, -2):
            begin(b1(n, 0, step))
        for way in (0, 1):
            begin(b2(n, way, 0, mx))

    def spread_near(n):
        for sign in (-1, 1):
            b1_wait(n, sign)
            for way in (0, 1):
                begin(b2(n, way, sign, mx))
        for sign in (-1, 1):
            b1_wait(n, 2 * sign)
            begin(b1(n, 2 * sign, -sign))
            begin(b1(n, 2 * sign, -2 * sign, half=0 if sign < 0 else 1))
            for way in (0, 1):
                begin(b2(n, way, 2 * sign, mx))

    def spread_far(n):
        for dz in (-3, 3):
            b1_wait(n, dz)
            for way in (0, 1):
                begin(b2(n, way, dz, mx))
        for half in (0, 1):
            b1_wait(n, 4, half=half)
        for way in (0, 1):
            begin(b2(n, way, 4, mx))

    order = (0, -1, 1, -2, 2, -3, 3, 4)

    def spread_across(n):
        for i, dz in enumerate(order):
            for way in (0, 1):
                source = x_of(2 * way - 1)
                b2(n, way, dz, source).wait_recv()
                if i % 2 == way:
                    begin(b3(n, way, dz, source))

    def spread_end(n):
        for i, dz in enumerate(order):
            b3(n, i % 2, dz, x_of(2)).wait_recv()

    def calibrate(n):
        @pl.loop(0, NX)
        def _(x):
            rows = pl.ds(pl.multiple_of(x * NZ * OWN, NZ * OWN), NZ * OWN)
            q = shared[n, x].reshape(NZ * OWN, 2 * APAD).astype(I32)
            for s in (0, 1):
                cols = slice(s * APAD, (s + 1) * APAD)
                part = q[:, cols]
                k = part[:, ANTENNA_COUNT:ANTENNA_COUNT + 1] - 15
                g = part.astype(F32) * jnp.exp2(k.astype(F32))
                high = g.astype(BF16)
                g_full[n, rows, cols] = g
                g_high[rows, cols] = high
                g_low[rows, cols] = (g - high.astype(F32)).astype(BF16)

        for s in (0, 1):
            cols = slice(s * APAD, (s + 1) * APAD)
            combo[s] = nt(select[s], g_high[:, cols]) + nt(select[s], g_low[:, cols])

        @pl.loop(1, NTA + 1)
        def _(j):
            d = time_peer(j)
            rows = pl.ds(pl.multiple_of(d * BASE, BASE), BASE)
            cols = slice(n * CW, (n + 1) * CW)
            u = amp[rows, cols].astype(F32) - combo[0, rows, :]
            v = ph[rows, cols].astype(F32) - combo[1, rows, :]
            magnitude = jnp.exp(u)
            sine, cosine = sin_cos(v)
            out_cal[n, d, 0] = (magnitude * cosine).astype(BF16)
            out_cal[n, d, 1] = (magnitude * sine).astype(BF16)

            @pl.when(j < NTA)
            def _():
                cal_copy(n, j).start()

        in_cal[n, 0] = out_cal[n, mt]

    def write_gains(n):
        for s in (0, 1):
            @pl.loop(0, CW // TILE)
            def _(k):
                rows = pl.ds(pl.multiple_of(k * TILE, TILE), TILE)
                block = g_full[n, rows, s * APAD:(s + 1) * APAD]
                start = s * ANTENNA_COUNT * NTILE + n * (CW // TILE) + k
                gains[pl.ds(start, ANTENNA_COUNT, stride=NTILE), :] = block.T[0:ANTENNA_COUNT]

    def mask(n):
        @pl.loop(0, NTA)
        def _(j):
            @pl.when(j > 0)
            def _():
                cal_copy(n, j).wait_recv()

            row = pl.multiple_of(lax.rem(mt - j + NTA, NTA) * LINE, LINE)
            w = keep[:, n * CW:(n + 1) * CW].astype(BF16)
            for c in (0, 1):
                masked[pl.ds(row + c * BASE, BASE), EDGE + n * CW:EDGE + (n + 1) * CW] = (
                    in_cal[n, j, c] * w
                )

    known = {2: 3 * PAIR, 3: 2 * PAIR, 4: PAIR}

    def fill_known():
        for p, size in known.items():
            early[p - 2] = nt(masked[:, p * PAIR:p * PAIR + size], wide[:, 0:size])

    def fill(low, high):
        for p in range(low, high):
            lane = p * PAIR
            size = known.get(p, 0) if high > 2 else 0
            stop = 3 * PAIR if p == NTILE // 2 - 1 else WINDOW
            rest = nt(masked[:, lane + size:lane + stop], wide[:, size:stop])
            mixed[...] = early[p - 2] + rest if size else rest

            @pl.loop(0, NT)
            def _(to):
                total = times[to, 0]
                value = times[to, 0] * mixed[0:LINE]
                for t in range(1, NT):
                    total = total + times[to, t]
                    value = value + times[to, t] * mixed[t * LINE:(t + 1) * LINE]
                ratio = rden[:, pl.ds(lane, PAIR)] * (1.0 / jnp.full((1, PAIR), total, F32))
                w = keep[:, pl.ds(lane, PAIR)]
                for c in (0, 1):
                    row = pl.multiple_of(to * LINE + c * BASE, BASE)
                    own = masked[pl.ds(row, BASE), pl.ds(lane + EDGE, PAIR)]
                    result = jnp.where(
                        w > 0.5, own.astype(F32), value[c * BASE:(c + 1) * BASE] * ratio
                    )
                    for i in (0, 1):
                        start = c * BASE * NTILE * NT + (2 * p + i) * NT + to
                        filled[pl.ds(start, BASE, stride=NTILE * NT), :] = (
                            result[:, i * TILE:(i + 1) * TILE]
                        )

    add_sums()
    solve()
    for n in range(PARTS):
        spread_start(n)
    spread_near(0)
    spread_near(1)
    spread_far(0)
    spread_near(2)
    spread_far(1)
    spread_across(0)
    spread_far(2)
    spread_across(1)
    spread_end(0)
    calibrate(0)
    spread_across(2)
    spread_end(1)
    calibrate(1)
    spread_end(2)
    calibrate(2)
    write_gains(0)
    mask(0)
    write_gains(1)
    mask(1)
    fill(0, 2)
    write_gains(2)
    fill_known()
    mask(2)
    fill(2, NTILE // 2)

    for copy in started:
        copy.wait_send()

    @pl.loop(1, NBL)
    def _(j):
        index_copy(j).wait_send()
        data_copy(j).wait_send()

    @pl.loop(1, NTA)
    def _(j):
        for n in range(PARTS):
            cal_copy(n, j).wait_send()


def calibrate_and_fill(amp, ph, group_row, couples, flags, times, channel, inverse):
    dma = pltpu.SemaphoreType.DMA
    vmem = pl.BlockSpec(memory_space=pltpu.VMEM)
    hbm = pl.BlockSpec(memory_space=pltpu.HBM)
    return pl.pallas_call(
        whole_kernel,
        name="calibrate_and_fill",
        out_shape=(
            jax.ShapeDtypeStruct((2 * ANTENNA_COUNT * NTILE, TILE), F32),
            jax.ShapeDtypeStruct((2 * BASE * NTILE * NT, TILE), F32),
        ),
        in_specs=[hbm] * 8,
        out_specs=(vmem, vmem),
        scratch_shapes=[
            pltpu.VMEM((ROWS, CH), BF16),
            pltpu.VMEM((ROWS, CH), BF16),
            pltpu.VMEM((1, ROWS), I32),
            pltpu.VMEM((2, ROWS), I32),
            pltpu.VMEM((NTILE, BASE), I32),
            pltpu.SMEM((NT, NT), F32),
            pltpu.VMEM((2 * REACH + 1, TILE, TILE), BF16),
            pltpu.VMEM((ANTENNA_COUNT, 2, ANTENNA_COUNT), F32),
            dma((8,)),
            pltpu.VMEM((NBL, 2 * MINE, ROWS), BF16),
            pltpu.VMEM((NBL, 2 * MINE, ROWS), BF16),
            pltpu.VMEM((8, 128), I16),
            pltpu.VMEM((NBL, 8, 128), I16),
            pltpu.VMEM((2, APAD, A8), F32),
            pltpu.VMEM((HOT, NGRP + 2 * MINE), F32),
            pltpu.VMEM((PARTS, NX, NZ, OWN, 2 * APAD), I16),
            pltpu.VMEM((PARTS, CW, 2 * APAD), F32),
            pltpu.VMEM((CW, 2 * APAD), BF16),
            pltpu.VMEM((CW, 2 * APAD), BF16),
            pltpu.VMEM((2, ROWS, APAD), BF16),
            pltpu.VMEM((2, ROWS, CW), F32),
            pltpu.VMEM((PAIR, WINDOW), BF16),
            pltpu.VMEM((BASE, CH), F32),
            pltpu.VMEM((BASE, CH + 2 * EDGE), BF16),
            pltpu.VMEM((NT * LINE, CH + 2 * EDGE), BF16),
            pltpu.VMEM((BASE, CH), F32),
            pltpu.VMEM((NT * LINE, PAIR), F32),
            pltpu.VMEM((3, NT * LINE, PAIR), F32),
            pltpu.VMEM((PARTS, NTA, 2, BASE, CW), BF16),
            pltpu.VMEM((PARTS, NTA, 2, BASE, CW), BF16),
            dma((NBL,)), dma((NBL,)), dma((NBL,)), dma((NBL,)),
            dma((PARTS, NZ)), dma((PARTS, NZ)), dma((PARTS, 2, NZ)), dma((PARTS, 2, NZ)),
            dma((PARTS, NZ)), dma((PARTS, NZ)), dma((PARTS, NTA)), dma((PARTS, NTA)),
        ],
        compiler_params=pltpu.CompilerParams(
            collective_id=0, has_side_effects=True, vmem_limit_bytes=40 * 2**20
        ),
    )(*(
        pltpu.with_memory_space_constraint(x, pltpu.HBM)
        for x in (amp, ph, group_row, couples, flags, times, channel, inverse)
    ))


def copy_kernel(a, b, out_a, out_b, sem):
    copies = []
    for k, (src, dst) in enumerate(((a, out_a), (b, out_b))):
        size = src.shape[0] // 2
        for i in range(2):
            rows = pl.ds(i * size, size)
            copies.append(pltpu.make_async_copy(src.at[rows], dst.at[rows], sem.at[k, i]))
    for copy in copies:
        copy.start()
    for copy in copies:
        copy.wait()


def copy_out(a, b):
    return pl.pallas_call(
        copy_kernel,
        name="copy_out",
        out_shape=(
            jax.ShapeDtypeStruct(a.shape, a.dtype), jax.ShapeDtypeStruct(b.shape, b.dtype)
        ),
        in_specs=[pl.BlockSpec(memory_space=pltpu.VMEM)] * 2,
        out_specs=(pl.BlockSpec(memory_space=pl.ANY),) * 2,
        scratch_shapes=[pltpu.SemaphoreType.DMA((2, 2))],
        compiler_params=pltpu.CompilerParams(vmem_limit_bytes=10 * 2**20),
    )(a, b)


def on_device(
    log_amplitude,
    phase,
    redundant_group_index,
    antenna_couples,
    tile_flag_mask,
    inverse,
    integration_kernel,
    channel_kernel,
):
    gains, filled = copy_out(*calibrate_and_fill(
        log_amplitude[:, 0], phase[:, 0], redundant_group_index[None, :], antenna_couples.T,
        tile_flag_mask.T, integration_kernel, channel_kernel, inverse.transpose(1, 0, 2),
    ))
    return (
        gains.reshape(2, ANTENNA_COUNT, 1, CH),
        filled.reshape(2, BASE, NTILE, NT, TILE).transpose(0, 1, 3, 2, 4).reshape(2, BASE, NT, CH),
    )


def solution(mesh):
    in_specs = (
        P("bl", "ta", None),
        P("bl", "ta", None),
        P("bl"),
        P("bl", None),
        P(("bl", "ta"), None),
        P(),
        P(),
        P(),
    )
    out_specs = (P(None, None, "ta", None), P(None, ("bl", "ta"), None, None))
    return jax.shard_map(
        on_device, mesh=mesh, in_specs=in_specs, out_specs=out_specs, check_vma=False
    )
```
